1024 devices in a mesh: dp: 32 (over y_hi, z, core), mp: 32 (over y_lo, x).
Axes of the slice: x: 8, y: 8 (y_hi: 2, y_lo: 4; y = y_hi * 4 + y_lo), z: 8, core: 2. Of those that a mesh axis runs over, the one named last changes fastest.
Arguments:
- visual: bfloat16 [256, 32, 6144], P('dp', None, 'mp'), may hold values from -6 to 6
- vis_gain: float32 [6144], replicated, may hold values from 0.1 to 1.9
- text: bfloat16 [256, 32, 4096], P(None, 'dp'), may hold values from -6 to 6
- text_gain: float32 [4096], replicated, may hold values from 0.1 to 1.9
- query_weight: bfloat16 [4096, 4096], P(None, 'mp'), may hold values from -0.375 to 0.375
- key_weight: bfloat16 [6144, 4096], P(None, 'mp'), may hold values from -0.078125 to 0.078125
- value_weight: bfloat16 [6144, 4096], P(None, 'mp'), may hold values from -0.078125 to 0.078125
- out_weight: bfloat16 [4096, 4096], P('mp'), may hold values from -0.09375 to 0.09375
Outputs:
- mixed: bfloat16 [256, 32, 4096], P('mp', 'dp')
The draws below stay inside these ranges and needn't reach their ends.
All inputs are finite; a program needn't handle non-finite values.
Results may differ from the reference program's by a relative error of at most 0.015.
Values may be sent and summed in bfloat16 or wider, within the bound.
No kernel may reach another device: no remote copies, remote signals or barrier semaphores. Data moves between devices by JAX's collectives and lax.ppermute only.
A program may use at most 32 MiB of HBM per device.

```python
import jax
import jax.numpy as jnp
from jax import lax

D_VIT = 6144
DEC = 4096
HEADS = 32
HEAD_DIM = 128
VIS = 256
TXT = 256
IMAGES = 32


def block_levels(stream_key, extent, pieces, low, high):
    def one(position, shards_of):
        heights = jax.random.uniform(jax.random.fold_in(jax.random.fold_in(stream_key, 6), position), (shards_of,), jnp.float32, low / len(pieces), high / len(pieces))
        return jnp.repeat(jnp.exp(heights), extent[position] // shards_of).reshape((-1,) + (1,) * (len(extent) - position - 1))

    factor_of = one(*pieces[0])
    for cut in pieces[1:]:
        factor_of = factor_of * one(*cut)
    return factor_of


def normal_values(stream_key, extent, width, bound, pieces=(), held_as=jnp.bfloat16):
    result = width * jax.random.normal(stream_key, extent, jnp.float32)
    if pieces:
        result = result * block_levels(stream_key, extent, pieces, -0.22, 0.18)
    return jnp.clip(result, -bound, bound).astype(held_as)


def setup_inputs(seed: int = 0) -> dict:
    key_of = jax.random.split(jax.random.key(seed), 9)
    visual = normal_values(key_of[0], (VIS, IMAGES, D_VIT), 1.0, 6.0, ((0, 32), (2, 32)))
    vis_gain = jnp.clip(1.0 + 0.18 * jax.random.normal(key_of[1], (D_VIT,), jnp.float32), 0.1, 1.9)
    text = normal_values(key_of[2], (TXT, IMAGES, DEC), 1.0, 6.0, ((1, 32),))
    text_gain = jnp.clip(1.0 + 0.18 * jax.random.normal(key_of[3], (DEC,), jnp.float32), 0.1, 1.9)
    query_weight = normal_values(key_of[4], (DEC, DEC), (DEC // 16) ** -0.5, 0.375, ((1, 32),))
    key_weight = normal_values(key_of[5], (D_VIT, DEC), D_VIT ** -0.5, 0.078125, ((1, 32),))
    value_weight = normal_values(key_of[6], (D_VIT, DEC), D_VIT ** -0.5, 0.078125, ((1, 32),))
    out_weight = normal_values(key_of[7], (DEC, DEC), DEC ** -0.5, 0.09375, ((0, 32),))
    return dict(visual=visual, vis_gain=vis_gain, text=text, text_gain=text_gain, query_weight=query_weight, key_weight=key_weight, value_weight=value_weight, out_weight=out_weight)


epsilon = 1e-06

def layer_norm(values, gain):
    average = lax.optimization_barrier(jnp.mean(values, axis=-1, keepdims=True))
    centred = values - average
    spread = lax.optimization_barrier(jnp.mean(centred * centred, axis=-1, keepdims=True))
    return centred * lax.rsqrt(spread + epsilon) * gain

def attend_image(operands):
    query_block, key_block, value_block = operands
    scores = jnp.einsum('thd,vhd->htv', query_block.astype(jnp.float32), key_block.astype(jnp.float32)) / jnp.sqrt(jnp.float32(HEAD_DIM))
    probs = jax.nn.softmax(scores, axis=-1).astype(jnp.bfloat16)
    return jnp.einsum('htv,vhd->thd', probs.astype(jnp.float32), value_block.astype(jnp.float32)).astype(jnp.bfloat16)

def reference(visual, vis_gain, text, text_gain, query_weight, key_weight, value_weight, out_weight):
    vis_norm = layer_norm(visual.astype(jnp.float32), vis_gain.astype(jnp.float32)).astype(jnp.bfloat16)
    flat_vis = vis_norm.reshape(VIS * IMAGES, D_VIT)
    keys = jnp.dot(flat_vis, key_weight, preferred_element_type=jnp.float32).astype(jnp.bfloat16)
    values = jnp.dot(flat_vis, value_weight, preferred_element_type=jnp.float32).astype(jnp.bfloat16)
    keys = keys.reshape(VIS, IMAGES, HEADS, HEAD_DIM).transpose(1, 0, 2, 3)
    values = values.reshape(VIS, IMAGES, HEADS, HEAD_DIM).transpose(1, 0, 2, 3)
    text_f = text.astype(jnp.float32)
    text_norm = (text_f * lax.rsqrt(lax.optimization_barrier(jnp.mean(text_f * text_f, axis=-1, keepdims=True)) + epsilon) * text_gain.astype(jnp.float32)).astype(jnp.bfloat16)
    queries = jnp.dot(text_norm.reshape(TXT * IMAGES, DEC), query_weight, preferred_element_type=jnp.float32).astype(jnp.bfloat16)
    queries = queries.reshape(TXT, IMAGES, HEADS, HEAD_DIM).transpose(1, 0, 2, 3)
    context = lax.map(attend_image, (queries, keys, values))
    context = context.transpose(1, 0, 2, 3).reshape(TXT * IMAGES, DEC)
    projected = jnp.dot(context, out_weight, preferred_element_type=jnp.float32).reshape(TXT, IMAGES, DEC)
    return (text_f + projected).astype(jnp.bfloat16)
```

```python
import jax
import jax.numpy as jnp
from jax import lax
from jax.sharding import Mesh
from jax.sharding import PartitionSpec as P


DEC = 4096
HEAD_DIM = 128
MP = ("mp_0", "mp_1")
SCALE = 8192.0

epsilon = 1e-06


def attend(visual, vis_gain, text, text_gain, query_weight, key_weight, value_weight, out_weight):
    rows, cols = lax.axis_size("mp_0"), lax.axis_size("mp_1")
    devices = rows * cols
    scaled = (visual.astype(jnp.float32) * SCALE).astype(jnp.float16)
    relayed = lax.all_to_all(scaled, "dp", split_axis=1, concat_axis=0, tiled=True)
    vis_tokens, _, features = relayed.shape
    block = relayed.reshape(vis_tokens, features).T
    column = lax.all_to_all(jnp.broadcast_to(block, (rows, features, vis_tokens)), "mp_0", 0, 0, tiled=True)
    row = lax.axis_index("mp_0")
    width = DEC // rows
    column, out_weight = lax.optimization_barrier((column, out_weight))
    out_rows = []
    for step in range(rows):
        chunk = lax.dynamic_slice_in_dim(out_weight, (row ^ step) * width, width, 1)
        out_rows.append(lax.ppermute(chunk, "mp_0", [(k, k ^ step) for k in range(rows)]) if step else chunk)
    whole = lax.all_gather(column.reshape(rows * features, vis_tokens), "mp_1", axis=0, tiled=True)
    whole = whole.reshape(cols, rows, features, vis_tokens).transpose(1, 0, 2, 3)
    whole = whole.reshape(devices * features, vis_tokens).astype(jnp.float32)
    centred = whole - jnp.mean(whole, axis=0, keepdims=True)
    spread = jnp.mean(centred * centred, axis=0, keepdims=True)
    normed = (centred * lax.rsqrt(spread + epsilon * SCALE * SCALE) * vis_gain[:, None]).astype(jnp.bfloat16)
    keys = lax.dot_general(
        normed, key_weight, (((0,), (0,)), ((), ())), preferred_element_type=jnp.float32
    ).astype(jnp.bfloat16)
    values = lax.dot_general(
        normed, value_weight, (((0,), (0,)), ((), ())), preferred_element_type=jnp.float32
    ).astype(jnp.bfloat16)
    text_tokens = text.shape[0]
    flat = text.reshape(text_tokens, DEC)
    text_f = flat.astype(jnp.float32)
    text_norm = (
        text_f * lax.rsqrt(jnp.mean(text_f * text_f, axis=-1, keepdims=True) + epsilon) * text_gain
    ).astype(jnp.bfloat16)
    queries = jnp.dot(text_norm, query_weight, preferred_element_type=jnp.float32).astype(jnp.bfloat16)
    scores = jnp.einsum("td,vd->tv", queries, keys, preferred_element_type=jnp.float32) / jnp.sqrt(
        jnp.float32(HEAD_DIM)
    )
    probs = jax.nn.softmax(scores, axis=-1).astype(jnp.bfloat16)
    context = jnp.einsum("tv,vd->td", probs, values, preferred_element_type=jnp.float32).astype(jnp.bfloat16)
    group = lax.all_to_all(jnp.broadcast_to(context, (rows, *context.shape)), "mp_0", 0, 0, tiled=True)
    group = jnp.concatenate([lax.dynamic_index_in_dim(group, row ^ k, 0, False) for k in range(rows)], axis=1)
    part = jnp.dot(group, jnp.concatenate(out_rows), preferred_element_type=jnp.float32).astype(jnp.bfloat16)
    tokens_here = text_tokens // devices
    parts = lax.all_to_all(part.reshape(devices, tokens_here, DEC // rows), MP, 0, 0, tiled=True)
    summed = jnp.sum(parts.reshape(rows, cols, tokens_here, DEC // rows).astype(jnp.float32), axis=1)
    summed = summed.transpose(1, 0, 2).reshape(tokens_here, DEC)
    residual = lax.dynamic_slice_in_dim(flat, lax.axis_index(MP) * tokens_here, tokens_here, 0)
    return (residual.astype(jnp.float32) + summed).astype(jnp.bfloat16).reshape(tokens_here, 1, DEC)


def solution(mesh):
    split = Mesh(mesh.devices.reshape(mesh.shape["dp"], 4, 8), ("dp", "mp_0", "mp_1"))
    in_specs = (
        P("dp", None, MP),
        P(),
        P(None, "dp", None),
        P(),
        P(None, MP),
        P(None, MP),
        P(None, MP),
        P(MP, None),
    )
    out_specs = P(MP, "dp", None)
    return jax.shard_map(attend, mesh=split, in_specs=in_specs, out_specs=out_specs, check_vma=False)
```

```python
import jax
import jax.numpy as jnp
from jax import lax
from jax.experimental import pallas as pl
from jax.experimental.pallas import tpu as pltpu
from jax.sharding import Mesh
from jax.sharding import PartitionSpec as P


DEC = 4096
HEAD_DIM = 128
DP = ("dp_0", "dp_1")
ROW = ("row_0", "row_1")
COL = ("col_0", "col_1")
MP = ROW + COL
QUAD = ("row_1", "col_1")
LANES = 128
CHUNK = 64
SCALE = 8192.0

epsilon = 1e-06


def attention_kernel(whole_ref, gain_ref, key_ref, value_ref, queries_ref, contexts_ref, normed_ref, scale_ref):
    cols, tokens, depth = whole_ref.shape
    rows = key_ref.shape[0] // cols
    count = cols * depth
    places = [(c, pl.ds(k, LANES)) for c in range(cols) for k in range(0, depth, LANES)]

    def normalize(step, carry):
        here = pl.ds(pl.multiple_of(step * CHUNK, CHUNK), CHUNK)
        sums = jnp.zeros((CHUNK, LANES), jnp.float32)
        for c, k in places:
            sums += whole_ref[c, here, k].astype(jnp.float32)
        mean = jnp.sum(sums, axis=1, keepdims=True) / count
        squares = jnp.zeros((CHUNK, LANES), jnp.float32)
        for c, k in places:
            centred = whole_ref[c, here, k].astype(jnp.float32) - mean
            squares += centred * centred
            normed_ref[c, here, k] = (centred * gain_ref[c : c + 1, k]).astype(jnp.bfloat16)
        spread = jnp.sum(squares, axis=1, keepdims=True) / count
        scale_ref[here, :] = jnp.broadcast_to(lax.rsqrt(spread + epsilon * SCALE * SCALE), (CHUNK, LANES))
        return carry

    lax.fori_loop(0, tokens // CHUNK, normalize, 0)
    projected = jnp.zeros((tokens, 2 * HEAD_DIM), jnp.float32)
    for c in range(cols):
        both = [jnp.concatenate([ref[r * cols + c] for r in range(rows)], axis=0) for ref in (key_ref, value_ref)]
        projected += jnp.dot(normed_ref[c], jnp.concatenate(both, axis=1), preferred_element_type=jnp.float32)
    keys = (projected[:, :HEAD_DIM] * scale_ref[...]).astype(jnp.bfloat16)
    values = (projected[:, HEAD_DIM:] * scale_ref[...]).astype(jnp.bfloat16)
    scores = lax.dot_general(queries_ref[...], keys, (((1,), (1,)), ((), ())), preferred_element_type=jnp.float32)
    scores *= HEAD_DIM**-0.5
    weights = jnp.exp(scores - jnp.max(scores, axis=1, keepdims=True))
    probs = (weights / jnp.sum(weights, axis=1, keepdims=True)).astype(jnp.bfloat16)
    context = jnp.dot(probs, values, preferred_element_type=jnp.float32).astype(jnp.bfloat16)
    for k in range(contexts_ref.shape[0]):
        contexts_ref[k] = context


def attend(visual, vis_gain, text, text_gain, query_weight, key_weight, value_weight, out_weight):
    rows, cols, quad = (lax.axis_size(a) for a in (ROW, COL, QUAD))
    halves, planes = (lax.axis_size(a) for a in DP)
    devices = rows * cols
    tokens, _, features = visual.shape
    text_tokens = text.shape[0]
    scaled = (visual.astype(jnp.float32) * SCALE).astype(jnp.float16)
    scaled = scaled.reshape(tokens, halves, planes, features).transpose(2, 1, 0, 3)
    relayed = lax.all_to_all(scaled, "dp_1", 0, 0, tiled=True)
    half_tokens = planes * tokens
    blocks = relayed.transpose(1, 3, 0, 2).reshape(halves, 1, features, half_tokens)
    blocks = jnp.broadcast_to(blocks, (halves, rows, features, half_tokens))
    column = lax.all_to_all(
        blocks.reshape(halves * rows, features, half_tokens), ("dp_0",) + ROW, 0, 0, tiled=True
    )
    member = lax.axis_index(QUAD)
    width = DEC // quad
    out_rows = []
    for step in range(quad):
        chunk = lax.dynamic_slice_in_dim(out_weight, (member ^ step) * width, width, 1)
        out_rows.append(lax.ppermute(chunk, QUAD, [(k, k ^ step) for k in range(quad)]) if step else chunk)
    column = column.reshape(halves, rows * features, half_tokens).transpose(0, 2, 1)
    column = column.reshape(halves * half_tokens, rows * features)
    whole = lax.all_gather(column, COL, axis=0, tiled=True)
    whole = whole.astype(jnp.bfloat16).reshape(cols, halves * half_tokens, rows * features)
    flat = text.reshape(text_tokens, DEC)
    text_f = flat.astype(jnp.float32)
    text_norm = (
        text_f * lax.rsqrt(jnp.mean(text_f * text_f, axis=-1, keepdims=True) + epsilon) * text_gain
    ).astype(jnp.bfloat16)
    queries = jnp.dot(text_norm, query_weight, preferred_element_type=jnp.float32).astype(jnp.bfloat16)
    gain = vis_gain.reshape(rows, cols, features).transpose(1, 0, 2).reshape(cols, rows * features)
    in_vmem = [
        pltpu.with_memory_space_constraint(v, pltpu.VMEM)
        for v in (
            whole,
            gain,
            key_weight.reshape(devices, features, HEAD_DIM),
            value_weight.reshape(devices, features, HEAD_DIM),
            queries,
        )
    ]
    contexts = pl.pallas_call(
        attention_kernel,
        out_shape=jax.ShapeDtypeStruct((quad, text_tokens, HEAD_DIM), jnp.bfloat16),
        in_specs=[pl.BlockSpec(memory_space=pltpu.VMEM)] * len(in_vmem),
        out_specs=pl.BlockSpec(memory_space=pltpu.VMEM),
        scratch_shapes=[
            pltpu.VMEM(whole.shape, jnp.bfloat16),
            pltpu.VMEM((whole.shape[1], LANES), jnp.float32),
        ],
        compiler_params=pltpu.CompilerParams(vmem_limit_bytes=12 << 20),
        name="attention",
    )(*in_vmem)
    group = lax.all_to_all(contexts, QUAD, 0, 0, tiled=True)
    group = jnp.concatenate([lax.dynamic_index_in_dim(group, member ^ k, 0, False) for k in range(quad)], axis=1)
    part = jnp.dot(group, jnp.concatenate(out_rows), preferred_element_type=jnp.float32).astype(jnp.bfloat16)
    tokens_here = text_tokens // devices
    parts = lax.all_to_all(part.reshape(devices, tokens_here, width), MP, 0, 0, tiled=True)
    parts = parts.reshape(*(lax.axis_size(a) for a in MP), tokens_here, width)
    summed = jnp.sum(parts.astype(jnp.float32), axis=(0, 2))
    summed = summed.transpose(2, 0, 1, 3).reshape(tokens_here, DEC)
    residual = lax.dynamic_slice_in_dim(flat, lax.axis_index(MP) * tokens_here, tokens_here, 0)
    return (residual.astype(jnp.float32) + summed).astype(jnp.bfloat16).reshape(tokens_here, 1, DEC)


def solution(mesh):
    split = Mesh(mesh.devices.reshape(2, mesh.shape["dp"] // 2, 2, 2, 4, 2), DP + MP)
    in_specs = (
        P(DP, None, MP),
        P(),
        P(None, DP, None),
        P(),
        P(None, MP),
        P(None, MP),
        P(None, MP),
        P(MP, None),
    )
    out_specs = P(MP, DP, None)
    return jax.shard_map(attend, mesh=split, in_specs=in_specs, out_specs=out_specs, check_vma=False)
```

```python
import jax
import jax.numpy as jnp
from jax import lax
from jax.experimental import pallas as pl
from jax.experimental.pallas import tpu as pltpu
from jax.sharding import Mesh
from jax.sharding import PartitionSpec as P


DEC = 4096
HEAD_DIM = 128
DP = ("dp_0", "dp_1")
ROW = ("row_0", "row_1")
COL = ("col_0", "col_1")
MP = ROW + COL
QUAD = ("row_1", "col_1")
LANES = 128
CHUNK = 64
SCALE = 8192.0

epsilon = 1e-06


def attention_kernel(
    whole_ref,
    gain_ref,
    queries_ref,
    key_hbm_ref,
    value_hbm_ref,
    contexts_ref,
    key_ref,
    value_ref,
    semaphores,
    normed_ref,
    scale_ref,
):
    key_copy = pltpu.make_async_copy(key_hbm_ref, key_ref, semaphores.at[0])
    value_copy = pltpu.make_async_copy(value_hbm_ref, value_ref, semaphores.at[1])
    key_copy.start()
    value_copy.start()
    cols, tokens, depth = whole_ref.shape
    rows = key_ref.shape[0] // cols
    count = cols * depth
    places = [(c, pl.ds(k, LANES)) for c in range(cols) for k in range(0, depth, LANES)]

    def normalize(step, carry):
        here = pl.ds(pl.multiple_of(step * CHUNK, CHUNK), CHUNK)
        sums = jnp.zeros((CHUNK, LANES), jnp.float32)
        for c, k in places:
            sums += whole_ref[c, here, k].astype(jnp.float32)
        mean = jnp.sum(sums, axis=1, keepdims=True) / count
        squares = jnp.zeros((CHUNK, LANES), jnp.float32)
        for c, k in places:
            centred = whole_ref[c, here, k].astype(jnp.float32) - mean
            squares += centred * centred
            normed_ref[c, here, k] = (centred * gain_ref[c : c + 1, k]).astype(jnp.bfloat16)
        spread = jnp.sum(squares, axis=1, keepdims=True) / count
        scale_ref[here, :] = jnp.broadcast_to(lax.rsqrt(spread + epsilon * SCALE * SCALE), (CHUNK, LANES))
        return carry

    lax.fori_loop(0, tokens // CHUNK, normalize, 0)
    key_copy.wait()
    value_copy.wait()
    projected = jnp.zeros((tokens, 2 * HEAD_DIM), jnp.float32)
    for c in range(cols):
        both = [jnp.concatenate([ref[r * cols + c] for r in range(rows)], axis=0) for ref in (key_ref, value_ref)]
        projected += jnp.dot(normed_ref[c], jnp.concatenate(both, axis=1), preferred_element_type=jnp.float32)
    keys = (projected[:, :HEAD_DIM] * scale_ref[...]).astype(jnp.bfloat16)
    values = (projected[:, HEAD_DIM:] * scale_ref[...]).astype(jnp.bfloat16)
    scores = lax.dot_general(queries_ref[...], keys, (((1,), (1,)), ((), ())), preferred_element_type=jnp.float32)
    scores *= HEAD_DIM**-0.5
    weights = jnp.exp(scores - jnp.max(scores, axis=1, keepdims=True))
    probs = (weights / jnp.sum(weights, axis=1, keepdims=True)).astype(jnp.bfloat16)
    context = jnp.dot(probs, values, preferred_element_type=jnp.float32).astype(jnp.bfloat16)
    for k in range(contexts_ref.shape[0]):
        contexts_ref[k] = context


def project_kernel(member_ref, group_ref, *refs):
    *chunk_refs, part_ref = refs
    part = jnp.zeros(part_ref.shape, jnp.float32)
    for k, chunk_ref in enumerate(chunk_refs):
        part += jnp.dot(group_ref[member_ref[0] ^ k], chunk_ref[...], preferred_element_type=jnp.float32)
    part_ref[...] = part.astype(jnp.bfloat16)


def finish_kernel(parts_ref, residual_ref, mixed_ref):
    row_0, row_1, col_0, col_1, _, width = parts_ref.shape
    for r in range(row_1):
        for c in range(col_1):
            here = pl.ds((r * col_1 + c) * width, width)
            total = residual_ref[:, here]
            for i in range(row_0):
                for j in range(col_0):
                    total += parts_ref[i, r, j, c].astype(jnp.float32)
            mixed_ref[:, here] = total.astype(jnp.bfloat16)


def in_vmem(value):
    return pltpu.with_memory_space_constraint(value, pltpu.VMEM)


def attend(visual, vis_gain, text, text_gain, query_weight, key_weight, value_weight, out_weight):
    rows, cols, quad = (lax.axis_size(a) for a in (ROW, COL, QUAD))
    halves, planes = (lax.axis_size(a) for a in DP)
    devices = rows * cols
    tokens, _, features = visual.shape
    text_tokens = text.shape[0]
    tokens_here = text_tokens // devices
    width = DEC // quad
    member = lax.axis_index(QUAD)
    relayed = visual.reshape(tokens, halves, planes, features).transpose(2, 1, 0, 3)
    relayed = lax.all_to_all(relayed, "dp_1", 0, 0, tiled=True)
    out_rows = []
    for step in range(quad):
        chunk = lax.dynamic_slice_in_dim(out_weight, (member ^ step) * width, width, 1)
        out_rows.append(lax.ppermute(chunk, QUAD, [(k, k ^ step) for k in range(quad)]) if step else chunk)
    half_tokens = planes * tokens
    blocks = relayed.transpose(1, 3, 0, 2).reshape(halves, 1, features, half_tokens)
    blocks = (blocks.astype(jnp.float32) * SCALE).astype(jnp.float16)
    blocks = jnp.broadcast_to(blocks, (halves, rows, features, half_tokens))
    blocks = blocks.reshape(halves * rows, features, half_tokens)
    column = lax.all_to_all(blocks, ("dp_0",) + ROW, 0, 0, tiled=True)
    flat = text.reshape(text_tokens, DEC)
    text_f = flat.astype(jnp.float32)
    text_norm = (
        text_f * lax.rsqrt(jnp.mean(text_f * text_f, axis=-1, keepdims=True) + epsilon) * text_gain
    ).astype(jnp.bfloat16)
    queries = jnp.dot(text_norm, query_weight, preferred_element_type=jnp.float32).astype(jnp.bfloat16)
    residual = lax.dynamic_slice_in_dim(flat, lax.axis_index(MP) * tokens_here, tokens_here, 0)
    residual = residual.astype(jnp.float32)
    gain = vis_gain.reshape(rows, cols, features).transpose(1, 0, 2).reshape(cols, rows * features)
    column = column.reshape(halves, rows * features, half_tokens).transpose(0, 2, 1)
    column = column.reshape(halves * half_tokens, rows * features)
    whole = lax.all_gather(column, COL, axis=0, tiled=True)
    whole = whole.astype(jnp.bfloat16).reshape(cols, halves * half_tokens, rows * features)
    operands = [in_vmem(v) for v in (whole, gain, queries)]
    operands += [w.reshape(devices, features, HEAD_DIM) for w in (key_weight, value_weight)]
    contexts = pl.pallas_call(
        attention_kernel,
        out_shape=jax.ShapeDtypeStruct((quad, text_tokens, HEAD_DIM), jnp.bfloat16),
        in_specs=[pl.BlockSpec(memory_space=pltpu.VMEM)] * 3 + [pl.BlockSpec(memory_space=pltpu.HBM)] * 2,
        out_specs=pl.BlockSpec(memory_space=pltpu.VMEM),
        scratch_shapes=[
            *(pltpu.VMEM(w.shape, jnp.bfloat16) for w in operands[3:]),
            pltpu.SemaphoreType.DMA((2,)),
            pltpu.VMEM(whole.shape, jnp.bfloat16),
            pltpu.VMEM((whole.shape[1], LANES), jnp.float32),
        ],
        compiler_params=pltpu.CompilerParams(vmem_limit_bytes=12 << 20),
        name="attention",
    )(*operands)
    group = lax.all_to_all(contexts, QUAD, 0, 0, tiled=True)
    operands = [in_vmem(v) for v in (group, *out_rows)]
    part = pl.pallas_call(
        project_kernel,
        out_shape=jax.ShapeDtypeStruct((text_tokens, width), jnp.bfloat16),
        in_specs=[pl.BlockSpec(memory_space=pltpu.SMEM)] + [pl.BlockSpec(memory_space=pltpu.VMEM)] * len(operands),
        out_specs=pl.BlockSpec(memory_space=pltpu.VMEM),
        compiler_params=pltpu.CompilerParams(vmem_limit_bytes=12 << 20),
        name="project",
    )(member.reshape(1), *operands)
    parts = lax.all_to_all(part.reshape(devices, tokens_here, width), MP, 0, 0, tiled=True)
    parts = parts.reshape(*(lax.axis_size(a) for a in MP), tokens_here, width)
    mixed = pl.pallas_call(
        finish_kernel,
        out_shape=jax.ShapeDtypeStruct((tokens_here, DEC), jnp.bfloat16),
        in_specs=[pl.BlockSpec(memory_space=pltpu.VMEM)] * 2,
        out_specs=pl.BlockSpec(memory_space=pltpu.VMEM),
        compiler_params=pltpu.CompilerParams(vmem_limit_bytes=12 << 20),
        name="finish",
    )(in_vmem(parts), in_vmem(residual))
    return mixed.reshape(tokens_here, 1, DEC)


def solution(mesh):
    split = Mesh(mesh.devices.reshape(2, mesh.shape["dp"] // 2, 2, 2, 4, 2), DP + MP)
    in_specs = (
        P(DP, None, MP),
        P(),
        P(None, DP, None),
        P(),
        P(None, MP),
        P(None, MP),
        P(None, MP),
        P(MP, None),
    )
    out_specs = P(MP, DP, None)
    return jax.shard_map(attend, mesh=split, in_specs=in_specs, out_specs=out_specs, check_vma=False)
```

```python
import jax
import jax.numpy as jnp
from jax import lax
from jax.experimental import pallas as pl
from jax.experimental.pallas import tpu as pltpu
from jax.sharding import Mesh
from jax.sharding import PartitionSpec as P


DEC = 4096
HEAD_DIM = 128
DP = ("dp_0", "dp_1")
ROW = ("row_0", "row_1")
COL = ("col_0", "col_1")
MP = ROW + COL
QUAD = ("row_1", "col_1")
LANES = 128
CHUNK = 64
SCALE = 8192.0

epsilon = 1e-06


def in_vmem(value):
    return pltpu.with_memory_space_constraint(value, pltpu.VMEM)


def in_hbm(value):
    return pltpu.with_memory_space_constraint(value, pltpu.HBM)


def attention_kernel(
    whole_ref,
    gain_ref,
    queries_ref,
    key_hbm_ref,
    value_hbm_ref,
    contexts_ref,
    key_ref,
    value_ref,
    semaphores,
    normed_ref,
    scale_ref,
):
    key_copy = pltpu.make_async_copy(key_hbm_ref, key_ref, semaphores.at[0])
    value_copy = pltpu.make_async_copy(value_hbm_ref, value_ref, semaphores.at[1])
    key_copy.start()
    value_copy.start()
    cols, tokens, depth = whole_ref.shape
    rows = key_ref.shape[0] // cols
    count = cols * depth
    places = [(c, pl.ds(k, LANES)) for c in range(cols) for k in range(0, depth, LANES)]

    def normalize(step, carry):
        here = pl.ds(pl.multiple_of(step * CHUNK, CHUNK), CHUNK)
        sums = jnp.zeros((CHUNK, LANES), jnp.float32)
        for c, k in places:
            sums += whole_ref[c, here, k].astype(jnp.float32)
        mean = jnp.sum(sums, axis=1, keepdims=True) / count
        squares = jnp.zeros((CHUNK, LANES), jnp.float32)
        for c, k in places:
            centred = whole_ref[c, here, k].astype(jnp.float32) - mean
            squares += centred * centred
            normed_ref[c, here, k] = (centred * gain_ref[c : c + 1, k]).astype(jnp.bfloat16)
        spread = jnp.sum(squares, axis=1, keepdims=True) / count
        scale_ref[here, :] = jnp.broadcast_to(lax.rsqrt(spread + epsilon * SCALE * SCALE), (CHUNK, LANES))
        return carry

    lax.fori_loop(0, tokens // CHUNK, normalize, 0)
    key_copy.wait()
    value_copy.wait()
    projected = jnp.zeros((tokens, 2 * HEAD_DIM), jnp.float32)
    for c in range(cols):
        both = [jnp.concatenate([ref[r * cols + c] for r in range(rows)], axis=0) for ref in (key_ref, value_ref)]
        projected += jnp.dot(normed_ref[c], jnp.concatenate(both, axis=1), preferred_element_type=jnp.float32)
    keys = (projected[:, :HEAD_DIM] * scale_ref[...]).astype(jnp.bfloat16)
    values = (projected[:, HEAD_DIM:] * scale_ref[...]).astype(jnp.bfloat16)
    scores = lax.dot_general(queries_ref[...], keys, (((1,), (1,)), ((), ())), preferred_element_type=jnp.float32)
    scores *= HEAD_DIM**-0.5
    weights = jnp.exp(scores - jnp.max(scores, axis=1, keepdims=True))
    probs = (weights / jnp.sum(weights, axis=1, keepdims=True)).astype(jnp.bfloat16)
    context = jnp.dot(probs, values, preferred_element_type=jnp.float32).astype(jnp.bfloat16)
    for k in range(contexts_ref.shape[0]):
        contexts_ref[k] = context


def pick_kernel(origins_ref, *refs):
    *source_refs, semaphores = refs
    picked_refs = source_refs[-(origins_ref.shape[0] // semaphores.shape[1]) :]
    source_refs = source_refs[: semaphores.shape[1]]
    copies = []
    for k, picked_ref in enumerate(picked_refs):
        for j, source_ref in enumerate(source_refs):
            origin = pl.multiple_of(origins_ref[k * len(source_refs) + j], picked_ref.shape[2])
            columns = source_ref.at[:, pl.ds(origin, picked_ref.shape[2])]
            copies.append(pltpu.make_async_copy(columns, picked_ref.at[j], semaphores.at[k, j]))
            copies[-1].start()
    for copy in copies:
        copy.wait()


def pick_columns(sources, origins, *shapes):
    return pl.pallas_call(
        pick_kernel,
        out_shape=shapes,
        in_specs=[pl.BlockSpec(memory_space=pltpu.SMEM)] + [pl.BlockSpec(memory_space=pl.ANY)] * len(sources),
        out_specs=[pl.BlockSpec(memory_space=pl.ANY)] * len(shapes),
        scratch_shapes=[pltpu.SemaphoreType.DMA((len(shapes), len(sources)))],
        compiler_params=pltpu.CompilerParams(vmem_limit_bytes=1 << 20),
        name="pick",
    )(jnp.stack(origins).astype(jnp.int32), in_hbm(sources[0]), *sources[1:])


def turn_kernel(column_ref, turned_ref):
    halves, _, half_tokens = column_ref.shape
    for h in range(halves):
        turned = column_ref[h].astype(jnp.float32).T
        turned_ref[pl.ds(h * half_tokens, half_tokens), :] = turned.astype(jnp.bfloat16)


def project_kernel(member_ref, group_ref, *refs):
    *chunk_refs, part_ref = refs
    part = jnp.zeros(part_ref.shape, jnp.float32)
    for across_x, chunk_ref in enumerate(chunk_refs):
        for across_y in range(chunk_ref.shape[0]):
            there = member_ref[0] ^ (2 * across_y + across_x)
            part += jnp.dot(group_ref[there], chunk_ref[across_y], preferred_element_type=jnp.float32)
    part_ref[...] = part.astype(jnp.bfloat16)


def finish_kernel(parts_ref, residual_ref, mixed_ref):
    row_0, row_1, col_0, col_1, _, width = parts_ref.shape
    for r in range(row_1):
        for c in range(col_1):
            here = pl.ds((r * col_1 + c) * width, width)
            total = residual_ref[:, here]
            for i in range(row_0):
                for j in range(col_0):
                    total += parts_ref[i, r, j, c].astype(jnp.float32)
            mixed_ref[:, here] = total.astype(jnp.bfloat16)


def attend(visual, vis_gain, text, text_gain, query_weight, key_weight, value_weight, out_weight):
    rows, cols, quad = (lax.axis_size(a) for a in (ROW, COL, QUAD))
    halves, planes = (lax.axis_size(a) for a in DP)
    devices = rows * cols
    tokens, _, features = visual.shape
    text_tokens = text.shape[0]
    tokens_here = text_tokens // devices
    width = DEC // quad
    member = lax.axis_index(QUAD)
    relayed = visual.reshape(tokens, halves, planes, features).transpose(2, 1, 0, 3)
    relayed = lax.all_to_all(relayed, "dp_1", 0, 0, tiled=True)
    row, col = (lax.axis_index(a) for a in QUAD)
    swap = [(0, 1), (1, 0)]
    half = DEC // 2
    quarter = jax.ShapeDtypeStruct((2, HEAD_DIM, width), jnp.bfloat16)
    send = pick_columns([out_weight], [(1 - row) * half], jax.ShapeDtypeStruct((1, HEAD_DIM, half), jnp.bfloat16))[0]
    beyond = lax.ppermute(send, QUAD[0], swap)[0]
    origins = [[row * half + c * width, c * width] for c in (col, 1 - col)]
    keep, send = pick_columns([out_weight, beyond], origins[0] + origins[1], quarter, quarter)
    out_rows = [keep, lax.ppermute(send, QUAD[1], swap)]
    half_tokens = planes * tokens
    blocks = relayed.transpose(1, 3, 0, 2).reshape(halves, 1, features, half_tokens)
    blocks = jnp.broadcast_to(blocks, (halves, rows, features, half_tokens))
    blocks = blocks.reshape(halves * rows, features, half_tokens)
    column = lax.all_to_all(blocks, ("dp_0",) + ROW, 0, 0, tiled=True)
    flat = text.reshape(text_tokens, DEC)
    text_f = flat.astype(jnp.float32)
    text_norm = (
        text_f * lax.rsqrt(jnp.mean(text_f * text_f, axis=-1, keepdims=True) + epsilon) * text_gain
    ).astype(jnp.bfloat16)
    queries = jnp.dot(text_norm, query_weight, preferred_element_type=jnp.float32).astype(jnp.bfloat16)
    residual = lax.dynamic_slice_in_dim(flat, lax.axis_index(MP) * tokens_here, tokens_here, 0)
    residual = residual.astype(jnp.float32)
    gain = vis_gain.reshape(rows, cols, features).transpose(1, 0, 2).reshape(cols, rows * features)
    column = pl.pallas_call(
        turn_kernel,
        out_shape=jax.ShapeDtypeStruct((halves * half_tokens, rows * features), jnp.bfloat16),
        in_specs=[pl.BlockSpec(memory_space=pltpu.VMEM)],
        out_specs=pl.BlockSpec(memory_space=pltpu.VMEM),
        compiler_params=pltpu.CompilerParams(vmem_limit_bytes=4 << 20),
        name="turn",
    )(in_vmem(column.reshape(halves, rows * features, half_tokens)))
    column = (column.astype(jnp.float32) * SCALE).astype(jnp.float16)
    whole = lax.all_gather(column, COL, axis=0, tiled=True)
    whole = whole.astype(jnp.bfloat16).reshape(cols, halves * half_tokens, rows * features)
    operands = [in_vmem(v) for v in (whole, gain, queries)]
    operands += [in_hbm(w.reshape(devices, features, HEAD_DIM)) for w in (key_weight, value_weight)]
    contexts = pl.pallas_call(
        attention_kernel,
        out_shape=jax.ShapeDtypeStruct((quad, text_tokens, HEAD_DIM), jnp.bfloat16),
        in_specs=[pl.BlockSpec(memory_space=pltpu.VMEM)] * 3 + [pl.BlockSpec(memory_space=pltpu.HBM)] * 2,
        out_specs=pl.BlockSpec(memory_space=pltpu.VMEM),
        scratch_shapes=[
            *(pltpu.VMEM(w.shape, jnp.bfloat16) for w in operands[3:]),
            pltpu.SemaphoreType.DMA((2,)),
            pltpu.VMEM(whole.shape, jnp.bfloat16),
            pltpu.VMEM((whole.shape[1], LANES), jnp.float32),
        ],
        compiler_params=pltpu.CompilerParams(vmem_limit_bytes=12 << 20),
        name="attention",
    )(*operands)
    group = lax.all_to_all(contexts, QUAD, 0, 0, tiled=True)
    operands = [in_vmem(v) for v in (group, *out_rows)]
    part = pl.pallas_call(
        project_kernel,
        out_shape=jax.ShapeDtypeStruct((text_tokens, width), jnp.bfloat16),
        in_specs=[pl.BlockSpec(memory_space=pltpu.SMEM)] + [pl.BlockSpec(memory_space=pltpu.VMEM)] * len(operands),
        out_specs=pl.BlockSpec(memory_space=pltpu.VMEM),
        compiler_params=pltpu.CompilerParams(vmem_limit_bytes=12 << 20),
        name="project",
    )(member.reshape(1), *operands)
    parts = lax.all_to_all(part.reshape(devices, tokens_here, width), MP, 0, 0, tiled=True)
    parts = parts.reshape(*(lax.axis_size(a) for a in MP), tokens_here, width)
    mixed = pl.pallas_call(
        finish_kernel,
        out_shape=jax.ShapeDtypeStruct((tokens_here, DEC), jnp.bfloat16),
        in_specs=[pl.BlockSpec(memory_space=pltpu.VMEM)] * 2,
        out_specs=pl.BlockSpec(memory_space=pltpu.VMEM),
        compiler_params=pltpu.CompilerParams(vmem_limit_bytes=12 << 20),
        name="finish",
    )(in_vmem(parts), in_vmem(residual))
    return mixed.reshape(tokens_here, 1, DEC)


def solution(mesh):
    split = Mesh(mesh.devices.reshape(2, mesh.shape["dp"] // 2, 2, 2, 4, 2), DP + MP)
    in_specs = (
        P(DP, None, MP),
        P(),
        P(None, DP, None),
        P(),
        P(None, MP),
        P(None, MP),
        P(None, MP),
        P(MP, None),
    )
    out_specs = P(MP, DP, None)
    return jax.shard_map(attend, mesh=split, in_specs=in_specs, out_specs=out_specs, check_vma=False)
```

```python
import jax
import jax.numpy as jnp
from jax import lax
from jax.experimental import pallas as pl
from jax.experimental.pallas import tpu as pltpu
from jax.sharding import Mesh
from jax.sharding import PartitionSpec as P


DEC = 4096
HEAD_DIM = 128
DP = ("dp_0", "dp_1")
ROW = ("row_0", "row_1")
COL = ("col_0", "col_1")
MP = ROW + COL
QUAD = ("row_1", "col_1")
LANES = 128
CHUNK = 64
TEXT_CHUNKS = 2
TEXT_BLOCK = 32
SCALE = 8192.0

epsilon = 1e-06


def in_vmem(value):
    return pltpu.with_memory_space_constraint(value, pltpu.VMEM)


def in_hbm(value):
    return pltpu.with_memory_space_constraint(value, pltpu.HBM)


def attention_kernel(
    whole_ref,
    gain_ref,
    queries_ref,
    key_hbm_ref,
    value_hbm_ref,
    contexts_ref,
    key_ref,
    value_ref,
    semaphores,
    normed_ref,
    scale_ref,
):
    key_copy = pltpu.make_async_copy(key_hbm_ref, key_ref, semaphores.at[0])
    value_copy = pltpu.make_async_copy(value_hbm_ref, value_ref, semaphores.at[1])
    key_copy.start()
    value_copy.start()
    cols, tokens, depth = whole_ref.shape
    rows = key_ref.shape[0] // cols
    count = cols * depth
    places = [(c, pl.ds(k, LANES)) for c in range(cols) for k in range(0, depth, LANES)]

    def normalize(step, carry):
        here = pl.ds(pl.multiple_of(step * CHUNK, CHUNK), CHUNK)
        sums = jnp.zeros((CHUNK, LANES), jnp.float32)
        for c, k in places:
            sums += whole_ref[c, here, k].astype(jnp.float32)
        mean = jnp.sum(sums, axis=1, keepdims=True) / count
        squares = jnp.zeros((CHUNK, LANES), jnp.float32)
        for c, k in places:
            centred = whole_ref[c, here, k].astype(jnp.float32) - mean
            squares += centred * centred
            normed_ref[c, here, k] = (centred * gain_ref[c : c + 1, k]).astype(jnp.bfloat16)
        spread = jnp.sum(squares, axis=1, keepdims=True) / count
        scale_ref[here, :] = jnp.broadcast_to(lax.rsqrt(spread + epsilon * SCALE * SCALE), (CHUNK, LANES))
        return carry

    lax.fori_loop(0, tokens // CHUNK, normalize, 0)
    key_copy.wait()
    value_copy.wait()
    projected = jnp.zeros((tokens, 2 * HEAD_DIM), jnp.float32)
    for c in range(cols):
        both = [jnp.concatenate([ref[r * cols + c] for r in range(rows)], axis=0) for ref in (key_ref, value_ref)]
        projected += jnp.dot(normed_ref[c], jnp.concatenate(both, axis=1), preferred_element_type=jnp.float32)
    keys = (projected[:, :HEAD_DIM] * scale_ref[...]).astype(jnp.bfloat16)
    values = (projected[:, HEAD_DIM:] * scale_ref[...]).astype(jnp.bfloat16)
    scores = lax.dot_general(queries_ref[...], keys, (((1,), (1,)), ((), ())), preferred_element_type=jnp.float32)
    scores *= HEAD_DIM**-0.5
    weights = jnp.exp(scores - jnp.max(scores, axis=1, keepdims=True))
    probs = (weights / jnp.sum(weights, axis=1, keepdims=True)).astype(jnp.bfloat16)
    context = jnp.dot(probs, values, preferred_element_type=jnp.float32).astype(jnp.bfloat16)
    for k in range(contexts_ref.shape[0]):
        contexts_ref[k] = context


def query_kernel(
    origin_ref,
    text_hbm_ref,
    weight_hbm_ref,
    gain_ref,
    queries_ref,
    residual_ref,
    text_ref,
    weight_ref,
    normed_ref,
    semaphores,
):
    tokens, width = text_ref.shape
    chunk = tokens // TEXT_CHUNKS
    places = [pl.ds(k * chunk, chunk) for k in range(TEXT_CHUNKS)]
    copies = [
        pltpu.make_async_copy(text_hbm_ref.at[here], text_ref.at[here], semaphores.at[k])
        for k, here in enumerate(places)
    ]
    copies.append(pltpu.make_async_copy(weight_hbm_ref, weight_ref, semaphores.at[TEXT_CHUNKS]))
    for copy in copies:
        copy.start()
    for k, here in enumerate(places):
        copies[k].wait()

        def normalize(step, carry, k=k):
            block = pl.ds(pl.multiple_of(step * TEXT_BLOCK, TEXT_BLOCK), TEXT_BLOCK)
            inside = pl.ds(pl.multiple_of(k * chunk + step * TEXT_BLOCK, TEXT_BLOCK), TEXT_BLOCK)
            squares = jnp.zeros((TEXT_BLOCK, LANES), jnp.float32)
            for n in range(0, width, LANES):
                x = text_ref[inside, pl.ds(n, LANES)].astype(jnp.float32)
                squares += x * x
            scale = lax.rsqrt(jnp.sum(squares, axis=1, keepdims=True) / width + epsilon)
            for n in range(0, width, LANES):
                x = text_ref[inside, pl.ds(n, LANES)].astype(jnp.float32)
                normed_ref[block, pl.ds(n, LANES)] = (x * scale * gain_ref[:, pl.ds(n, LANES)]).astype(jnp.bfloat16)
            return carry

        lax.fori_loop(0, chunk // TEXT_BLOCK, normalize, 0)
        if k == 0:
            copies[-1].wait()
        queries_ref[here, :] = jnp.dot(
            normed_ref[...], weight_ref[...], preferred_element_type=jnp.float32
        ).astype(jnp.bfloat16)
    count = residual_ref.shape[0]
    pair = text_ref[pl.ds(pl.multiple_of(origin_ref[0] // 16 * 16, 16), 16), :].astype(jnp.float32)
    residual_ref[...] = jnp.where(origin_ref[0] % 16 == 0, pair[:count], pair[count:])


def pick_kernel(origins_ref, *refs):
    *source_refs, semaphores = refs
    picked_refs = source_refs[-(origins_ref.shape[0] // semaphores.shape[1]) :]
    source_refs = source_refs[: semaphores.shape[1]]
    copies = []
    for k, picked_ref in enumerate(picked_refs):
        for j, source_ref in enumerate(source_refs):
            origin = pl.multiple_of(origins_ref[k * len(source_refs) + j], picked_ref.shape[2])
            columns = source_ref.at[:, pl.ds(origin, picked_ref.shape[2])]
            copies.append(pltpu.make_async_copy(columns, picked_ref.at[j], semaphores.at[k, j]))
            copies[-1].start()
    for copy in copies:
        copy.wait()


def pick_columns(sources, origins, *shapes):
    return pl.pallas_call(
        pick_kernel,
        out_shape=shapes,
        in_specs=[pl.BlockSpec(memory_space=pltpu.SMEM)] + [pl.BlockSpec(memory_space=pl.ANY)] * len(sources),
        out_specs=[pl.BlockSpec(memory_space=pl.ANY)] * len(shapes),
        scratch_shapes=[pltpu.SemaphoreType.DMA((len(shapes), len(sources)))],
        compiler_params=pltpu.CompilerParams(vmem_limit_bytes=1 << 20),
        name="pick",
    )(jnp.stack(origins).astype(jnp.int32), in_hbm(sources[0]), *sources[1:])


def turn_kernel(column_ref, turned_ref):
    halves, _, half_tokens = column_ref.shape
    for h in range(halves):
        turned = column_ref[h].astype(jnp.float32).T
        turned_ref[pl.ds(h * half_tokens, half_tokens), :] = turned.astype(jnp.bfloat16)


def project_kernel(member_ref, group_ref, *refs):
    *chunk_refs, part_ref = refs
    part = jnp.zeros(part_ref.shape, jnp.float32)
    for across_x, chunk_ref in enumerate(chunk_refs):
        for across_y in range(chunk_ref.shape[0]):
            there = member_ref[0] ^ (2 * across_y + across_x)
            part += jnp.dot(group_ref[there], chunk_ref[across_y], preferred_element_type=jnp.float32)
    part_ref[...] = part.astype(jnp.bfloat16)


def finish_kernel(parts_ref, residual_ref, mixed_ref):
    row_0, row_1, col_0, col_1, _, width = parts_ref.shape
    for r in range(row_1):
        for c in range(col_1):
            here = pl.ds((r * col_1 + c) * width, width)
            total = residual_ref[:, here]
            for i in range(row_0):
                for j in range(col_0):
                    total += parts_ref[i, r, j, c].astype(jnp.float32)
            mixed_ref[:, here] = total.astype(jnp.bfloat16)


def attend(visual, vis_gain, text, text_gain, query_weight, key_weight, value_weight, out_weight):
    rows, cols, quad = (lax.axis_size(a) for a in (ROW, COL, QUAD))
    halves, planes = (lax.axis_size(a) for a in DP)
    devices = rows * cols
    tokens, _, features = visual.shape
    text_tokens = text.shape[0]
    tokens_here = text_tokens // devices
    width = DEC // quad
    member = lax.axis_index(QUAD)
    relayed = visual.reshape(tokens, halves, planes, features).transpose(2, 1, 0, 3)
    relayed = lax.all_to_all(relayed, "dp_1", 0, 0, tiled=True)
    row, col = (lax.axis_index(a) for a in QUAD)
    swap = [(0, 1), (1, 0)]
    half = DEC // 2
    quarter = jax.ShapeDtypeStruct((2, HEAD_DIM, width), jnp.bfloat16)
    send = pick_columns([out_weight], [(1 - row) * half], jax.ShapeDtypeStruct((1, HEAD_DIM, half), jnp.bfloat16))[0]
    beyond = lax.ppermute(send, QUAD[0], swap)[0]
    origins = [[row * half + c * width, c * width] for c in (col, 1 - col)]
    keep, send = pick_columns([out_weight, beyond], origins[0] + origins[1], quarter, quarter)
    out_rows = [keep, lax.ppermute(send, QUAD[1], swap)]
    half_tokens = planes * tokens
    blocks = relayed.transpose(1, 3, 0, 2).reshape(halves, 1, features, half_tokens)
    blocks = jnp.broadcast_to(blocks, (halves, rows, features, half_tokens))
    blocks = blocks.reshape(halves * rows, features, half_tokens)
    column = lax.all_to_all(blocks, ("dp_0",) + ROW, 0, 0, tiled=True)
    flat = text.reshape(text_tokens, DEC)
    queries, residual = pl.pallas_call(
        query_kernel,
        out_shape=(
            jax.ShapeDtypeStruct((text_tokens, HEAD_DIM), jnp.bfloat16),
            jax.ShapeDtypeStruct((tokens_here, DEC), jnp.float32),
        ),
        in_specs=[pl.BlockSpec(memory_space=pltpu.SMEM)]
        + [pl.BlockSpec(memory_space=pl.ANY)] * 2
        + [pl.BlockSpec(memory_space=pltpu.VMEM)],
        out_specs=[pl.BlockSpec(memory_space=pltpu.VMEM)] * 2,
        scratch_shapes=[
            pltpu.VMEM(flat.shape, jnp.bfloat16),
            pltpu.VMEM(query_weight.shape, jnp.bfloat16),
            pltpu.VMEM((text_tokens // TEXT_CHUNKS, DEC), jnp.bfloat16),
            pltpu.SemaphoreType.DMA((TEXT_CHUNKS + 1,)),
        ],
        compiler_params=pltpu.CompilerParams(vmem_limit_bytes=8 << 20),
        name="query",
    )(
        (lax.axis_index(MP) * tokens_here).reshape(1),
        in_hbm(flat),
        in_hbm(query_weight),
        text_gain.reshape(1, DEC),
    )
    gain = vis_gain.reshape(rows, cols, features).transpose(1, 0, 2).reshape(cols, rows * features)
    column = pl.pallas_call(
        turn_kernel,
        out_shape=jax.ShapeDtypeStruct((halves * half_tokens, rows * features), jnp.bfloat16),
        in_specs=[pl.BlockSpec(memory_space=pltpu.VMEM)],
        out_specs=pl.BlockSpec(memory_space=pltpu.VMEM),
        compiler_params=pltpu.CompilerParams(vmem_limit_bytes=4 << 20),
        name="turn",
    )(in_vmem(column.reshape(halves, rows * features, half_tokens)))
    column = (column.astype(jnp.float32) * SCALE).astype(jnp.float16)
    whole = lax.all_gather(column, COL, axis=0, tiled=True)
    whole = whole.astype(jnp.bfloat16).reshape(cols, halves * half_tokens, rows * features)
    operands = [in_vmem(v) for v in (whole, gain, queries)]
    operands += [in_hbm(w.reshape(devices, features, HEAD_DIM)) for w in (key_weight, value_weight)]
    contexts = pl.pallas_call(
        attention_kernel,
        out_shape=jax.ShapeDtypeStruct((quad, text_tokens, HEAD_DIM), jnp.bfloat16),
        in_specs=[pl.BlockSpec(memory_space=pltpu.VMEM)] * 3 + [pl.BlockSpec(memory_space=pltpu.HBM)] * 2,
        out_specs=pl.BlockSpec(memory_space=pltpu.VMEM),
        scratch_shapes=[
            *(pltpu.VMEM(w.shape, jnp.bfloat16) for w in operands[3:]),
            pltpu.SemaphoreType.DMA((2,)),
            pltpu.VMEM(whole.shape, jnp.bfloat16),
            pltpu.VMEM((whole.shape[1], LANES), jnp.float32),
        ],
        compiler_params=pltpu.CompilerParams(vmem_limit_bytes=12 << 20),
        name="attention",
    )(*operands)
    group = lax.all_to_all(contexts, QUAD, 0, 0, tiled=True)
    operands = [in_vmem(v) for v in (group, *out_rows)]
    part = pl.pallas_call(
        project_kernel,
        out_shape=jax.ShapeDtypeStruct((text_tokens, width), jnp.bfloat16),
        in_specs=[pl.BlockSpec(memory_space=pltpu.SMEM)] + [pl.BlockSpec(memory_space=pltpu.VMEM)] * len(operands),
        out_specs=pl.BlockSpec(memory_space=pltpu.VMEM),
        compiler_params=pltpu.CompilerParams(vmem_limit_bytes=12 << 20),
        name="project",
    )(member.reshape(1), *operands)
    parts = lax.all_to_all(part.reshape(devices, tokens_here, width), MP, 0, 0, tiled=True)
    parts = parts.reshape(*(lax.axis_size(a) for a in MP), tokens_here, width)
    mixed = pl.pallas_call(
        finish_kernel,
        out_shape=jax.ShapeDtypeStruct((tokens_here, DEC), jnp.bfloat16),
        in_specs=[pl.BlockSpec(memory_space=pltpu.VMEM)] * 2,
        out_specs=pl.BlockSpec(memory_space=pltpu.VMEM),
        compiler_params=pltpu.CompilerParams(vmem_limit_bytes=12 << 20),
        name="finish",
    )(in_vmem(parts), in_vmem(residual))
    return mixed.reshape(tokens_here, 1, DEC)


def solution(mesh):
    split = Mesh(mesh.devices.reshape(2, mesh.shape["dp"] // 2, 2, 2, 4, 2), DP + MP)
    in_specs = (
        P(DP, None, MP),
        P(),
        P(None, DP, None),
        P(),
        P(None, MP),
        P(None, MP),
        P(None, MP),
        P(MP, None),
    )
    out_specs = P(MP, DP, None)
    return jax.shard_map(attend, mesh=split, in_specs=in_specs, out_specs=out_specs, check_vma=False)
```

```python
import jax
import jax.numpy as jnp
from jax import lax
from jax.experimental import pallas as pl
from jax.experimental.pallas import tpu as pltpu
from jax.sharding import Mesh
from jax.sharding import PartitionSpec as P


DEC = 4096
HEAD_DIM = 128
DP = ("dp_0", "dp_1")
ROW = ("row_0", "row_1")
COL = ("col_0", "col_1")
MP = ROW + COL
QUAD = ("row_1", "col_1")
LANES = 128
CHUNK = 64
TEXT_CHUNKS = 2
TEXT_BLOCK = 32
SCALE = 8192.0

epsilon = 1e-06


def in_vmem(value):
    return pltpu.with_memory_space_constraint(value, pltpu.VMEM)


def in_hbm(value):
    return pltpu.with_memory_space_constraint(value, pltpu.HBM)


def attention_kernel(
    whole_ref,
    gain_ref,
    queries_ref,
    key_hbm_ref,
    value_hbm_ref,
    contexts_ref,
    key_ref,
    value_ref,
    semaphores,
    normed_ref,
    scale_ref,
):
    key_copy = pltpu.make_async_copy(key_hbm_ref, key_ref, semaphores.at[0])
    value_copy = pltpu.make_async_copy(value_hbm_ref, value_ref, semaphores.at[1])
    key_copy.start()
    value_copy.start()
    cols, tokens, depth = whole_ref.shape
    rows = key_ref.shape[0] // cols
    count = cols * depth
    places = [(c, pl.ds(k, LANES)) for c in range(cols) for k in range(0, depth, LANES)]

    def normalize(step, carry):
        here = pl.ds(pl.multiple_of(step * CHUNK, CHUNK), CHUNK)
        sums = jnp.zeros((CHUNK, LANES), jnp.float32)
        for c, k in places:
            sums += whole_ref[c, here, k].astype(jnp.float32)
        mean = jnp.sum(sums, axis=1, keepdims=True) / count
        squares = jnp.zeros((CHUNK, LANES), jnp.float32)
        for c, k in places:
            centred = whole_ref[c, here, k].astype(jnp.float32) - mean
            squares += centred * centred
            normed_ref[c, here, k] = (centred * gain_ref[c : c + 1, k]).astype(jnp.bfloat16)
        spread = jnp.sum(squares, axis=1, keepdims=True) / count
        scale_ref[here, :] = jnp.broadcast_to(lax.rsqrt(spread + epsilon * SCALE * SCALE), (CHUNK, LANES))
        return carry

    lax.fori_loop(0, tokens // CHUNK, normalize, 0)
    key_copy.wait()
    value_copy.wait()
    projected = jnp.zeros((tokens, 2 * HEAD_DIM), jnp.float32)
    for c in range(cols):
        both = [jnp.concatenate([ref[r * cols + c] for r in range(rows)], axis=0) for ref in (key_ref, value_ref)]
        projected += jnp.dot(normed_ref[c], jnp.concatenate(both, axis=1), preferred_element_type=jnp.float32)
    keys = (projected[:, :HEAD_DIM] * scale_ref[...]).astype(jnp.bfloat16)
    values = (projected[:, HEAD_DIM:] * scale_ref[...]).astype(jnp.bfloat16)
    scores = lax.dot_general(queries_ref[...], keys, (((1,), (1,)), ((), ())), preferred_element_type=jnp.float32)
    scores *= HEAD_DIM**-0.5
    weights = jnp.exp(scores - jnp.max(scores, axis=1, keepdims=True))
    probs = (weights / jnp.sum(weights, axis=1, keepdims=True)).astype(jnp.bfloat16)
    context = jnp.dot(probs, values, preferred_element_type=jnp.float32).astype(jnp.bfloat16)
    for k in range(contexts_ref.shape[0]):
        contexts_ref[k] = context


def query_kernel(
    origin_ref,
    text_hbm_ref,
    weight_hbm_ref,
    gain_ref,
    queries_ref,
    residual_ref,
    text_ref,
    weight_ref,
    normed_ref,
    semaphores,
):
    tokens, width = text_ref.shape
    chunk = tokens // TEXT_CHUNKS
    places = [pl.ds(k * chunk, chunk) for k in range(TEXT_CHUNKS)]
    copies = [
        pltpu.make_async_copy(text_hbm_ref.at[here], text_ref.at[here], semaphores.at[k])
        for k, here in enumerate(places)
    ]
    copies.append(pltpu.make_async_copy(weight_hbm_ref, weight_ref, semaphores.at[TEXT_CHUNKS]))
    for copy in copies:
        copy.start()
    for k, here in enumerate(places):
        copies[k].wait()

        def normalize(step, carry, k=k):
            block = pl.ds(pl.multiple_of(step * TEXT_BLOCK, TEXT_BLOCK), TEXT_BLOCK)
            inside = pl.ds(pl.multiple_of(k * chunk + step * TEXT_BLOCK, TEXT_BLOCK), TEXT_BLOCK)
            squares = jnp.zeros((TEXT_BLOCK, LANES), jnp.float32)
            for n in range(0, width, LANES):
                x = text_ref[inside, pl.ds(n, LANES)].astype(jnp.float32)
                squares += x * x
            scale = lax.rsqrt(jnp.sum(squares, axis=1, keepdims=True) / width + epsilon)
            for n in range(0, width, LANES):
                x = text_ref[inside, pl.ds(n, LANES)].astype(jnp.float32)
                normed_ref[block, pl.ds(n, LANES)] = (x * scale * gain_ref[:, pl.ds(n, LANES)]).astype(jnp.bfloat16)
            return carry

        lax.fori_loop(0, chunk // TEXT_BLOCK, normalize, 0)
        if k == 0:
            copies[-1].wait()
        queries_ref[here, :] = jnp.dot(
            normed_ref[...], weight_ref[...], preferred_element_type=jnp.float32
        ).astype(jnp.bfloat16)
    count = residual_ref.shape[0]
    pair = text_ref[pl.ds(pl.multiple_of(origin_ref[0] // 16 * 16, 16), 16), :].astype(jnp.float32)
    residual_ref[...] = jnp.where(origin_ref[0] % 16 == 0, pair[:count], pair[count:])


def pick_kernel(origins_ref, *refs):
    *source_refs, semaphores = refs
    picked_refs = source_refs[-(origins_ref.shape[0] // semaphores.shape[1]) :]
    source_refs = source_refs[: semaphores.shape[1]]
    copies = []
    for k, picked_ref in enumerate(picked_refs):
        for j, source_ref in enumerate(source_refs):
            origin = pl.multiple_of(origins_ref[k * len(source_refs) + j], picked_ref.shape[2])
            columns = source_ref.at[:, pl.ds(origin, picked_ref.shape[2])]
            copies.append(pltpu.make_async_copy(columns, picked_ref.at[j], semaphores.at[k, j]))
            copies[-1].start()
    for copy in copies:
        copy.wait()


def pick_columns(sources, origins, *shapes):
    return pl.pallas_call(
        pick_kernel,
        out_shape=shapes,
        in_specs=[pl.BlockSpec(memory_space=pltpu.SMEM)] + [pl.BlockSpec(memory_space=pl.ANY)] * len(sources),
        out_specs=[pl.BlockSpec(memory_space=pl.ANY)] * len(shapes),
        scratch_shapes=[pltpu.SemaphoreType.DMA((len(shapes), len(sources)))],
        compiler_params=pltpu.CompilerParams(vmem_limit_bytes=1 << 20),
        name="pick",
    )(jnp.stack(origins).astype(jnp.int32), in_hbm(sources[0]), *sources[1:])


def deal_kernel(visual_ref, dealt_ref):
    planes, halves = dealt_ref.shape[:2]
    dealt = jnp.swapaxes(visual_ref[...].astype(jnp.float32), 0, 1).astype(jnp.bfloat16)
    for h in range(halves):
        for p in range(planes):
            dealt_ref[p, h] = dealt[h * planes + p]


def spread_kernel(relayed_ref, blocks_ref):
    planes, halves, tokens, features = relayed_ref.shape
    copies = blocks_ref.shape[0] // halves
    for h in range(halves):
        block = relayed_ref[:, h].astype(jnp.float32).reshape(planes * tokens, features).T.astype(jnp.bfloat16)
        for k in range(copies):
            blocks_ref[h * copies + k] = block


def turn_kernel(column_ref, turned_ref):
    halves, _, half_tokens = column_ref.shape
    for h in range(halves):
        turned = column_ref[h].astype(jnp.float32).T
        turned_ref[pl.ds(h * half_tokens, half_tokens), :] = turned.astype(jnp.bfloat16)


def project_kernel(member_ref, group_ref, *refs):
    *chunk_refs, part_ref = refs
    part = jnp.zeros(part_ref.shape, jnp.float32)
    for across_y, chunk_ref in enumerate(chunk_refs):
        for across_x in range(chunk_ref.shape[0]):
            there = member_ref[0] ^ (2 * across_y + across_x)
            part += jnp.dot(group_ref[there], chunk_ref[across_x], preferred_element_type=jnp.float32)
    part_ref[...] = part.astype(jnp.bfloat16)


def finish_kernel(parts_ref, residual_ref, mixed_ref):
    row_0, row_1, col_0, col_1, _, width = parts_ref.shape
    for r in range(row_1):
        for c in range(col_1):
            here = pl.ds((c * row_1 + r) * width, width)
            total = residual_ref[:, here]
            for i in range(row_0):
                for j in range(col_0):
                    total += parts_ref[i, r, j, c].astype(jnp.float32)
            mixed_ref[:, here] = total.astype(jnp.bfloat16)


def attend(visual, vis_gain, text, text_gain, query_weight, key_weight, value_weight, out_weight):
    rows, cols, quad = (lax.axis_size(a) for a in (ROW, COL, QUAD))
    halves, planes = (lax.axis_size(a) for a in DP)
    devices = rows * cols
    tokens, _, features = visual.shape
    text_tokens = text.shape[0]
    tokens_here = text_tokens // devices
    width = DEC // quad
    member = lax.axis_index(QUAD)
    relayed = pl.pallas_call(
        deal_kernel,
        out_shape=jax.ShapeDtypeStruct((planes, halves, tokens, features), jnp.bfloat16),
        in_specs=[pl.BlockSpec(memory_space=pltpu.VMEM)],
        out_specs=pl.BlockSpec(memory_space=pltpu.VMEM),
        compiler_params=pltpu.CompilerParams(vmem_limit_bytes=4 << 20),
        name="deal",
    )(visual)
    relayed = lax.all_to_all(relayed, "dp_1", 0, 0, tiled=True)
    row, col = (lax.axis_index(a) for a in QUAD)
    swap = [(0, 1), (1, 0)]
    half = DEC // 2
    quarter = jax.ShapeDtypeStruct((2, HEAD_DIM, width), jnp.bfloat16)
    send = pick_columns([out_weight], [(1 - col) * half], jax.ShapeDtypeStruct((1, HEAD_DIM, half), jnp.bfloat16))[0]
    beyond = lax.ppermute(send, QUAD[1], swap)[0]
    origins = [[col * half + r * width, r * width] for r in (row, 1 - row)]
    keep, send = pick_columns([out_weight, beyond], origins[0] + origins[1], quarter, quarter)
    out_rows = [keep, lax.ppermute(send, QUAD[0], swap)]
    half_tokens = planes * tokens
    blocks = pl.pallas_call(
        spread_kernel,
        out_shape=jax.ShapeDtypeStruct((halves * rows, features, half_tokens), jnp.bfloat16),
        in_specs=[pl.BlockSpec(memory_space=pltpu.VMEM)],
        out_specs=pl.BlockSpec(memory_space=pltpu.VMEM),
        compiler_params=pltpu.CompilerParams(vmem_limit_bytes=4 << 20),
        name="spread",
    )(in_vmem(relayed))
    column = lax.all_to_all(blocks, ("dp_0",) + ROW, 0, 0, tiled=True)
    flat = text.reshape(text_tokens, DEC)
    queries, residual = pl.pallas_call(
        query_kernel,
        out_shape=(
            jax.ShapeDtypeStruct((text_tokens, HEAD_DIM), jnp.bfloat16),
            jax.ShapeDtypeStruct((tokens_here, DEC), jnp.float32),
        ),
        in_specs=[pl.BlockSpec(memory_space=pltpu.SMEM)]
        + [pl.BlockSpec(memory_space=pl.ANY)] * 2
        + [pl.BlockSpec(memory_space=pltpu.VMEM)],
        out_specs=[pl.BlockSpec(memory_space=pltpu.VMEM)] * 2,
        scratch_shapes=[
            pltpu.VMEM(flat.shape, jnp.bfloat16),
            pltpu.VMEM(query_weight.shape, jnp.bfloat16),
            pltpu.VMEM((text_tokens // TEXT_CHUNKS, DEC), jnp.bfloat16),
            pltpu.SemaphoreType.DMA((TEXT_CHUNKS + 1,)),
        ],
        compiler_params=pltpu.CompilerParams(vmem_limit_bytes=8 << 20),
        name="query",
    )(
        (lax.axis_index(MP) * tokens_here).reshape(1),
        in_hbm(flat),
        in_hbm(query_weight),
        text_gain.reshape(1, DEC),
    )
    gain = vis_gain.reshape(rows, cols, features).transpose(1, 0, 2).reshape(cols, rows * features)
    column = pl.pallas_call(
        turn_kernel,
        out_shape=jax.ShapeDtypeStruct((halves * half_tokens, rows * features), jnp.bfloat16),
        in_specs=[pl.BlockSpec(memory_space=pltpu.VMEM)],
        out_specs=pl.BlockSpec(memory_space=pltpu.VMEM),
        compiler_params=pltpu.CompilerParams(vmem_limit_bytes=4 << 20),
        name="turn",
    )(in_vmem(column.reshape(halves, rows * features, half_tokens)))
    column = (column.astype(jnp.float32) * SCALE).astype(jnp.float16)
    whole = lax.all_gather(column, COL, axis=0, tiled=True)
    whole = whole.astype(jnp.bfloat16).reshape(cols, halves * half_tokens, rows * features)
    operands = [in_vmem(v) for v in (whole, gain, queries)]
    operands += [in_hbm(w.reshape(devices, features, HEAD_DIM)) for w in (key_weight, value_weight)]
    contexts = pl.pallas_call(
        attention_kernel,
        out_shape=jax.ShapeDtypeStruct((quad, text_tokens, HEAD_DIM), jnp.bfloat16),
        in_specs=[pl.BlockSpec(memory_space=pltpu.VMEM)] * 3 + [pl.BlockSpec(memory_space=pltpu.HBM)] * 2,
        out_specs=pl.BlockSpec(memory_space=pltpu.VMEM),
        scratch_shapes=[
            *(pltpu.VMEM(w.shape, jnp.bfloat16) for w in operands[3:]),
            pltpu.SemaphoreType.DMA((2,)),
            pltpu.VMEM(whole.shape, jnp.bfloat16),
            pltpu.VMEM((whole.shape[1], LANES), jnp.float32),
        ],
        compiler_params=pltpu.CompilerParams(vmem_limit_bytes=12 << 20),
        name="attention",
    )(*operands)
    group = lax.all_to_all(contexts, QUAD, 0, 0, tiled=True)
    operands = [in_vmem(v) for v in (group, *out_rows)]
    part = pl.pallas_call(
        project_kernel,
        out_shape=jax.ShapeDtypeStruct((text_tokens, width), jnp.bfloat16),
        in_specs=[pl.BlockSpec(memory_space=pltpu.SMEM)] + [pl.BlockSpec(memory_space=pltpu.VMEM)] * len(operands),
        out_specs=pl.BlockSpec(memory_space=pltpu.VMEM),
        compiler_params=pltpu.CompilerParams(vmem_limit_bytes=12 << 20),
        name="project",
    )(member.reshape(1), *operands)
    parts = lax.all_to_all(part.reshape(devices, tokens_here, width), MP, 0, 0, tiled=True)
    parts = parts.reshape(*(lax.axis_size(a) for a in MP), tokens_here, width)
    mixed = pl.pallas_call(
        finish_kernel,
        out_shape=jax.ShapeDtypeStruct((tokens_here, DEC), jnp.bfloat16),
        in_specs=[pl.BlockSpec(memory_space=pltpu.VMEM)] * 2,
        out_specs=pl.BlockSpec(memory_space=pltpu.VMEM),
        compiler_params=pltpu.CompilerParams(vmem_limit_bytes=12 << 20),
        name="finish",
    )(in_vmem(parts), in_vmem(residual))
    return mixed.reshape(tokens_here, 1, DEC)


def solution(mesh):
    split = Mesh(mesh.devices.reshape(2, mesh.shape["dp"] // 2, 2, 2, 4, 2), DP + MP)
    in_specs = (
        P(DP, None, MP),
        P(),
        P(None, DP, None),
        P(),
        P(None, MP),
        P(None, MP),
        P(None, MP),
        P(MP, None),
    )
    out_specs = P(MP, DP, None)
    return jax.shard_map(attend, mesh=split, in_specs=in_specs, out_specs=out_specs, check_vma=False)
```

```python
import jax
import jax.numpy as jnp
from jax import lax
from jax.experimental import pallas as pl
from jax.experimental.pallas import tpu as pltpu
from jax.sharding import Mesh
from jax.sharding import PartitionSpec as P


DEC = 4096
HEAD_DIM = 128
ROW = ("row_0", "row_1")
COL = ("col_0", "col_1")
MP = ROW + COL
QUAD = ("row_1", "col_1")
LANES = 128
CHUNK = 64
TEXT_CHUNKS = 2
TEXT_BLOCK = 32
SCALE = 8192.0

epsilon = 1e-06


def in_vmem(value):
    return pltpu.with_memory_space_constraint(value, pltpu.VMEM)


def in_hbm(value):
    return pltpu.with_memory_space_constraint(value, pltpu.HBM)


def attention_kernel(
    whole_ref,
    gain_ref,
    queries_ref,
    key_hbm_ref,
    value_hbm_ref,
    contexts_ref,
    key_ref,
    value_ref,
    semaphores,
    normed_ref,
    scale_ref,
):
    key_copy = pltpu.make_async_copy(key_hbm_ref, key_ref, semaphores.at[0])
    value_copy = pltpu.make_async_copy(value_hbm_ref, value_ref, semaphores.at[1])
    key_copy.start()
    value_copy.start()
    cols, tokens, depth = whole_ref.shape
    rows = key_ref.shape[0] // cols
    count = cols * depth
    places = [(c, pl.ds(k, LANES)) for c in range(cols) for k in range(0, depth, LANES)]

    def normalize(step, carry):
        here = pl.ds(pl.multiple_of(step * CHUNK, CHUNK), CHUNK)
        sums = jnp.zeros((CHUNK, LANES), jnp.float32)
        for c, k in places:
            sums += whole_ref[c, here, k].astype(jnp.float32)
        mean = jnp.sum(sums, axis=1, keepdims=True) / count
        squares = jnp.zeros((CHUNK, LANES), jnp.float32)
        for c, k in places:
            centred = whole_ref[c, here, k].astype(jnp.float32) - mean
            squares += centred * centred
            normed_ref[c, here, k] = (centred * gain_ref[c : c + 1, k]).astype(jnp.bfloat16)
        spread = jnp.sum(squares, axis=1, keepdims=True) / count
        scale_ref[here, :] = jnp.broadcast_to(lax.rsqrt(spread + epsilon * SCALE * SCALE), (CHUNK, LANES))
        return carry

    lax.fori_loop(0, tokens // CHUNK, normalize, 0)
    key_copy.wait()
    value_copy.wait()
    projected = jnp.zeros((tokens, 2 * HEAD_DIM), jnp.float32)
    for c in range(cols):
        both = [jnp.concatenate([ref[r * cols + c] for r in range(rows)], axis=0) for ref in (key_ref, value_ref)]
        projected += jnp.dot(normed_ref[c], jnp.concatenate(both, axis=1), preferred_element_type=jnp.float32)
    keys = (projected[:, :HEAD_DIM] * scale_ref[...]).astype(jnp.bfloat16)
    values = (projected[:, HEAD_DIM:] * scale_ref[...]).astype(jnp.bfloat16)
    scores = lax.dot_general(queries_ref[...], keys, (((1,), (1,)), ((), ())), preferred_element_type=jnp.float32)
    scores *= HEAD_DIM**-0.5
    weights = jnp.exp(scores - jnp.max(scores, axis=1, keepdims=True))
    probs = (weights / jnp.sum(weights, axis=1, keepdims=True)).astype(jnp.bfloat16)
    context = jnp.dot(probs, values, preferred_element_type=jnp.float32).astype(jnp.bfloat16)
    for k in range(contexts_ref.shape[0]):
        contexts_ref[k] = context


def query_kernel(
    origin_ref,
    text_hbm_ref,
    weight_hbm_ref,
    gain_ref,
    queries_ref,
    residual_ref,
    text_ref,
    weight_ref,
    normed_ref,
    semaphores,
):
    tokens, width = text_ref.shape
    chunk = tokens // TEXT_CHUNKS
    places = [pl.ds(k * chunk, chunk) for k in range(TEXT_CHUNKS)]
    copies = [
        pltpu.make_async_copy(text_hbm_ref.at[here], text_ref.at[here], semaphores.at[k])
        for k, here in enumerate(places)
    ]
    copies.append(pltpu.make_async_copy(weight_hbm_ref, weight_ref, semaphores.at[TEXT_CHUNKS]))
    for copy in copies:
        copy.start()
    for k, here in enumerate(places):
        copies[k].wait()

        def normalize(step, carry, k=k):
            block = pl.ds(pl.multiple_of(step * TEXT_BLOCK, TEXT_BLOCK), TEXT_BLOCK)
            inside = pl.ds(pl.multiple_of(k * chunk + step * TEXT_BLOCK, TEXT_BLOCK), TEXT_BLOCK)
            squares = jnp.zeros((TEXT_BLOCK, LANES), jnp.float32)
            for n in range(0, width, LANES):
                x = text_ref[inside, pl.ds(n, LANES)].astype(jnp.float32)
                squares += x * x
            scale = lax.rsqrt(jnp.sum(squares, axis=1, keepdims=True) / width + epsilon)
            for n in range(0, width, LANES):
                x = text_ref[inside, pl.ds(n, LANES)].astype(jnp.float32)
                normed_ref[block, pl.ds(n, LANES)] = (x * scale * gain_ref[:, pl.ds(n, LANES)]).astype(jnp.bfloat16)
            return carry

        lax.fori_loop(0, chunk // TEXT_BLOCK, normalize, 0)
        if k == 0:
            copies[-1].wait()
        queries_ref[here, :] = jnp.dot(
            normed_ref[...], weight_ref[...], preferred_element_type=jnp.float32
        ).astype(jnp.bfloat16)
    count = residual_ref.shape[0]
    pair = text_ref[pl.ds(pl.multiple_of(origin_ref[0] // 16 * 16, 16), 16), :].astype(jnp.float32)
    residual_ref[...] = jnp.where(origin_ref[0] % 16 == 0, pair[:count], pair[count:])


def pick_kernel(origins_ref, *refs):
    *source_refs, semaphores = refs
    picked_refs = source_refs[-(origins_ref.shape[0] // semaphores.shape[1]) :]
    source_refs = source_refs[: semaphores.shape[1]]
    copies = []
    for k, picked_ref in enumerate(picked_refs):
        for j, source_ref in enumerate(source_refs):
            origin = pl.multiple_of(origins_ref[k * len(source_refs) + j], picked_ref.shape[2])
            columns = source_ref.at[:, pl.ds(origin, picked_ref.shape[2])]
            copies.append(pltpu.make_async_copy(columns, picked_ref.at[j], semaphores.at[k, j]))
            copies[-1].start()
    for copy in copies:
        copy.wait()


def pick_columns(sources, origins, *shapes):
    return pl.pallas_call(
        pick_kernel,
        out_shape=shapes,
        in_specs=[pl.BlockSpec(memory_space=pltpu.SMEM)] + [pl.BlockSpec(memory_space=pl.ANY)] * len(sources),
        out_specs=[pl.BlockSpec(memory_space=pl.ANY)] * len(shapes),
        scratch_shapes=[pltpu.SemaphoreType.DMA((len(shapes), len(sources)))],
        compiler_params=pltpu.CompilerParams(vmem_limit_bytes=1 << 20),
        name="pick",
    )(jnp.stack(origins).astype(jnp.int32), in_hbm(sources[0]), *sources[1:])


def deal_kernel(visual_ref, dealt_ref):
    dealt_ref[...] = jnp.swapaxes(visual_ref[...].astype(jnp.float32), 0, 1).astype(jnp.bfloat16)


def spread_kernel(relayed_ref, blocks_ref):
    images, tokens, features = relayed_ref.shape
    block = relayed_ref[...].astype(jnp.float32).reshape(images * tokens, features).T.astype(jnp.bfloat16)
    for k in range(blocks_ref.shape[0]):
        blocks_ref[k] = block


def turn_kernel(column_ref, turned_ref):
    turned_ref[...] = column_ref[...].astype(jnp.float32).T.astype(jnp.bfloat16)


def project_kernel(member_ref, group_ref, *refs):
    *chunk_refs, part_ref = refs
    part = jnp.zeros(part_ref.shape, jnp.float32)
    for across_y, chunk_ref in enumerate(chunk_refs):
        for across_x in range(chunk_ref.shape[0]):
            there = member_ref[0] ^ (2 * across_y + across_x)
            part += jnp.dot(group_ref[there], chunk_ref[across_x], preferred_element_type=jnp.float32)
    part_ref[...] = part.astype(jnp.bfloat16)


def finish_kernel(parts_ref, residual_ref, mixed_ref):
    row_0, row_1, col_0, col_1, _, width = parts_ref.shape
    for r in range(row_1):
        for c in range(col_1):
            here = pl.ds((c * row_1 + r) * width, width)
            total = residual_ref[:, here]
            for i in range(row_0):
                for j in range(col_0):
                    total += parts_ref[i, r, j, c].astype(jnp.float32)
            mixed_ref[:, here] = total.astype(jnp.bfloat16)


def attend(visual, vis_gain, text, text_gain, query_weight, key_weight, value_weight, out_weight):
    rows, cols, quad = (lax.axis_size(a) for a in (ROW, COL, QUAD))
    images = lax.axis_size("dp")
    devices = rows * cols
    tokens, _, features = visual.shape
    text_tokens = text.shape[0]
    tokens_here = text_tokens // devices
    width = DEC // quad
    member = lax.axis_index(QUAD)
    relayed = pl.pallas_call(
        deal_kernel,
        out_shape=jax.ShapeDtypeStruct((images, tokens, features), jnp.bfloat16),
        in_specs=[pl.BlockSpec(memory_space=pltpu.VMEM)],
        out_specs=pl.BlockSpec(memory_space=pltpu.VMEM),
        compiler_params=pltpu.CompilerParams(vmem_limit_bytes=4 << 20),
        name="deal",
    )(visual)
    relayed = lax.all_to_all(relayed, "dp", 0, 0, tiled=True)
    row, col = (lax.axis_index(a) for a in QUAD)
    swap = [(0, 1), (1, 0)]
    half = DEC // 2
    quarter = jax.ShapeDtypeStruct((2, HEAD_DIM, width), jnp.bfloat16)
    send = pick_columns([out_weight], [(1 - col) * half], jax.ShapeDtypeStruct((1, HEAD_DIM, half), jnp.bfloat16))[0]
    beyond = lax.ppermute(send, QUAD[1], swap)[0]
    origins = [[col * half + r * width, r * width] for r in (row, 1 - row)]
    keep, send = pick_columns([out_weight, beyond], origins[0] + origins[1], quarter, quarter)
    out_rows = [keep, lax.ppermute(send, QUAD[0], swap)]
    vis_tokens = images * tokens
    blocks = pl.pallas_call(
        spread_kernel,
        out_shape=jax.ShapeDtypeStruct((rows, features, vis_tokens), jnp.bfloat16),
        in_specs=[pl.BlockSpec(memory_space=pltpu.VMEM)],
        out_specs=pl.BlockSpec(memory_space=pltpu.VMEM),
        compiler_params=pltpu.CompilerParams(vmem_limit_bytes=4 << 20),
        name="spread",
    )(in_vmem(relayed))
    column = lax.all_to_all(blocks, ROW, 0, 0, tiled=True)
    flat = text.reshape(text_tokens, DEC)
    queries, residual = pl.pallas_call(
        query_kernel,
        out_shape=(
            jax.ShapeDtypeStruct((text_tokens, HEAD_DIM), jnp.bfloat16),
            jax.ShapeDtypeStruct((tokens_here, DEC), jnp.float32),
        ),
        in_specs=[pl.BlockSpec(memory_space=pltpu.SMEM)]
        + [pl.BlockSpec(memory_space=pl.ANY)] * 2
        + [pl.BlockSpec(memory_space=pltpu.VMEM)],
        out_specs=[pl.BlockSpec(memory_space=pltpu.VMEM)] * 2,
        scratch_shapes=[
            pltpu.VMEM(flat.shape, jnp.bfloat16),
            pltpu.VMEM(query_weight.shape, jnp.bfloat16),
            pltpu.VMEM((text_tokens // TEXT_CHUNKS, DEC), jnp.bfloat16),
            pltpu.SemaphoreType.DMA((TEXT_CHUNKS + 1,)),
        ],
        compiler_params=pltpu.CompilerParams(vmem_limit_bytes=8 << 20),
        name="query",
    )(
        (lax.axis_index(MP) * tokens_here).reshape(1),
        in_hbm(flat),
        in_hbm(query_weight),
        text_gain.reshape(1, DEC),
    )
    gain = vis_gain.reshape(rows, cols, features).transpose(1, 0, 2).reshape(cols, rows * features)
    column = pl.pallas_call(
        turn_kernel,
        out_shape=jax.ShapeDtypeStruct((vis_tokens, rows * features), jnp.bfloat16),
        in_specs=[pl.BlockSpec(memory_space=pltpu.VMEM)],
        out_specs=pl.BlockSpec(memory_space=pltpu.VMEM),
        compiler_params=pltpu.CompilerParams(vmem_limit_bytes=4 << 20),
        name="turn",
    )(in_vmem(column.reshape(rows * features, vis_tokens)))
    column = (column.astype(jnp.float32) * SCALE).astype(jnp.float16)
    whole = lax.all_gather(column, COL, axis=0, tiled=True)
    whole = whole.astype(jnp.bfloat16).reshape(cols, vis_tokens, rows * features)
    operands = [in_vmem(v) for v in (whole, gain, queries)]
    operands += [in_hbm(w.reshape(devices, features, HEAD_DIM)) for w in (key_weight, value_weight)]
    contexts = pl.pallas_call(
        attention_kernel,
        out_shape=jax.ShapeDtypeStruct((quad, text_tokens, HEAD_DIM), jnp.bfloat16),
        in_specs=[pl.BlockSpec(memory_space=pltpu.VMEM)] * 3 + [pl.BlockSpec(memory_space=pltpu.HBM)] * 2,
        out_specs=pl.BlockSpec(memory_space=pltpu.VMEM),
        scratch_shapes=[
            *(pltpu.VMEM(w.shape, jnp.bfloat16) for w in operands[3:]),
            pltpu.SemaphoreType.DMA((2,)),
            pltpu.VMEM(whole.shape, jnp.bfloat16),
            pltpu.VMEM((whole.shape[1], LANES), jnp.float32),
        ],
        compiler_params=pltpu.CompilerParams(vmem_limit_bytes=12 << 20),
        name="attention",
    )(*operands)
    group = lax.all_to_all(contexts, QUAD, 0, 0, tiled=True)
    operands = [in_vmem(v) for v in (group, *out_rows)]
    part = pl.pallas_call(
        project_kernel,
        out_shape=jax.ShapeDtypeStruct((text_tokens, width), jnp.bfloat16),
        in_specs=[pl.BlockSpec(memory_space=pltpu.SMEM)] + [pl.BlockSpec(memory_space=pltpu.VMEM)] * len(operands),
        out_specs=pl.BlockSpec(memory_space=pltpu.VMEM),
        compiler_params=pltpu.CompilerParams(vmem_limit_bytes=12 << 20),
        name="project",
    )(member.reshape(1), *operands)
    parts = lax.all_to_all(part.reshape(devices, tokens_here, width), MP, 0, 0, tiled=True)
    parts = parts.reshape(*(lax.axis_size(a) for a in MP), tokens_here, width)
    mixed = pl.pallas_call(
        finish_kernel,
        out_shape=jax.ShapeDtypeStruct((tokens_here, DEC), jnp.bfloat16),
        in_specs=[pl.BlockSpec(memory_space=pltpu.VMEM)] * 2,
        out_specs=pl.BlockSpec(memory_space=pltpu.VMEM),
        compiler_params=pltpu.CompilerParams(vmem_limit_bytes=12 << 20),
        name="finish",
    )(in_vmem(parts), in_vmem(residual))
    return mixed.reshape(tokens_here, 1, DEC)


def solution(mesh):
    split = Mesh(mesh.devices.reshape(mesh.shape["dp"], 2, 2, 4, 2), ("dp",) + MP)
    in_specs = (
        P("dp", None, MP),
        P(),
        P(None, "dp", None),
        P(),
        P(None, MP),
        P(None, MP),
        P(None, MP),
        P(MP, None),
    )
    out_specs = P(MP, "dp", None)
    return jax.shard_map(attend, mesh=split, in_specs=in_specs, out_specs=out_specs, check_vma=False)
```

```python
import jax
import jax.numpy as jnp
from jax import lax
from jax.experimental import pallas as pl
from jax.experimental.pallas import tpu as pltpu
from jax.sharding import Mesh
from jax.sharding import PartitionSpec as P


DEC = 4096
HEAD_DIM = 128
ROW = ("row_0", "row_1")
COL = ("col_0", "col_1")
MP = ROW + COL
QUAD = ("row_1", "col_1")
LANES = 128
CHUNK = 64
TEXT_CHUNKS = 2
TEXT_BLOCK = 32
SCALE = 8192.0

epsilon = 1e-06


def in_vmem(value):
    return pltpu.with_memory_space_constraint(value, pltpu.VMEM)


def in_hbm(value):
    return pltpu.with_memory_space_constraint(value, pltpu.HBM)


def attention_kernel(
    whole_ref,
    gain_ref,
    queries_ref,
    key_hbm_ref,
    value_hbm_ref,
    contexts_ref,
    key_ref,
    value_ref,
    semaphores,
    normed_ref,
    mean_ref,
    square_ref,
):
    cols, tokens, depth = whole_ref.shape
    rows = key_ref.shape[0]
    count = cols * depth
    copies = [
        [
            pltpu.make_async_copy(source.at[:, c], target.at[:, c], semaphores.at[k, c])
            for k, (source, target) in enumerate(((key_hbm_ref, key_ref), (value_hbm_ref, value_ref)))
        ]
        for c in range(cols)
    ]
    for pair in copies:
        for copy in pair:
            copy.start()

    def average(step, carry):
        here = pl.ds(pl.multiple_of(step * CHUNK, CHUNK), CHUNK)
        sums = jnp.zeros((CHUNK, LANES), jnp.float32)
        for c in range(cols):
            for k in range(0, depth, LANES):
                sums += whole_ref[c, here, pl.ds(k, LANES)].astype(jnp.float32)
        mean_ref[here, :] = jnp.broadcast_to(jnp.sum(sums, axis=1, keepdims=True) / count, (CHUNK, LANES))
        return carry

    lax.fori_loop(0, tokens // CHUNK, average, 0)
    projected = jnp.zeros((tokens, 2 * HEAD_DIM), jnp.float32)
    for c in range(cols):
        for t in range(0, tokens, CHUNK):
            here = pl.ds(t, CHUNK)
            mean = mean_ref[here, :]
            squares = square_ref[here, :] if c else jnp.zeros((CHUNK, LANES), jnp.float32)
            for k in range(0, depth, LANES):
                centred = whole_ref[c, here, pl.ds(k, LANES)].astype(jnp.float32) - mean
                squares += centred * centred
                normed_ref[c, here, pl.ds(k, LANES)] = (centred * gain_ref[c : c + 1, pl.ds(k, LANES)]).astype(
                    jnp.bfloat16
                )
            square_ref[here, :] = squares
        for copy in copies[c]:
            copy.wait()
        both = [jnp.concatenate([ref[r, c] for r in range(rows)], axis=0) for ref in (key_ref, value_ref)]
        projected += jnp.dot(normed_ref[c], jnp.concatenate(both, axis=1), preferred_element_type=jnp.float32)
    spread = jnp.sum(square_ref[...], axis=1, keepdims=True) / count
    scale = lax.rsqrt(spread + epsilon * SCALE * SCALE)
    keys = (projected[:, :HEAD_DIM] * scale).astype(jnp.bfloat16)
    values = (projected[:, HEAD_DIM:] * scale).astype(jnp.bfloat16)
    scores = lax.dot_general(queries_ref[...], keys, (((1,), (1,)), ((), ())), preferred_element_type=jnp.float32)
    scores *= HEAD_DIM**-0.5
    weights = jnp.exp(scores - jnp.max(scores, axis=1, keepdims=True))
    probs = (weights / jnp.sum(weights, axis=1, keepdims=True)).astype(jnp.bfloat16)
    context = jnp.dot(probs, values, preferred_element_type=jnp.float32).astype(jnp.bfloat16)
    for k in range(contexts_ref.shape[0]):
        contexts_ref[k] = context


def query_kernel(
    origin_ref,
    text_hbm_ref,
    weight_hbm_ref,
    gain_ref,
    queries_ref,
    residual_ref,
    text_ref,
    weight_ref,
    normed_ref,
    semaphores,
):
    tokens, width = text_ref.shape
    chunk = tokens // TEXT_CHUNKS
    places = [pl.ds(k * chunk, chunk) for k in range(TEXT_CHUNKS)]
    copies = [
        pltpu.make_async_copy(text_hbm_ref.at[here], text_ref.at[here], semaphores.at[k])
        for k, here in enumerate(places)
    ]
    copies.append(pltpu.make_async_copy(weight_hbm_ref, weight_ref, semaphores.at[TEXT_CHUNKS]))
    for copy in copies:
        copy.start()
    for k, here in enumerate(places):
        copies[k].wait()

        def normalize(step, carry, k=k):
            block = pl.ds(pl.multiple_of(step * TEXT_BLOCK, TEXT_BLOCK), TEXT_BLOCK)
            inside = pl.ds(pl.multiple_of(k * chunk + step * TEXT_BLOCK, TEXT_BLOCK), TEXT_BLOCK)
            squares = jnp.zeros((TEXT_BLOCK, LANES), jnp.float32)
            for n in range(0, width, LANES):
                x = text_ref[inside, pl.ds(n, LANES)].astype(jnp.float32)
                squares += x * x
            scale = lax.rsqrt(jnp.sum(squares, axis=1, keepdims=True) / width + epsilon)
            for n in range(0, width, LANES):
                x = text_ref[inside, pl.ds(n, LANES)].astype(jnp.float32)
                normed_ref[block, pl.ds(n, LANES)] = (x * scale * gain_ref[:, pl.ds(n, LANES)]).astype(jnp.bfloat16)
            return carry

        lax.fori_loop(0, chunk // TEXT_BLOCK, normalize, 0)
        if k == 0:
            copies[-1].wait()
        queries_ref[here, :] = jnp.dot(
            normed_ref[...], weight_ref[...], preferred_element_type=jnp.float32
        ).astype(jnp.bfloat16)
    count = residual_ref.shape[0]
    pair = text_ref[pl.ds(pl.multiple_of(origin_ref[0] // 16 * 16, 16), 16), :].astype(jnp.float32)
    residual_ref[...] = jnp.where(origin_ref[0] % 16 == 0, pair[:count], pair[count:])


def pick_kernel(origins_ref, *refs):
    *source_refs, semaphores = refs
    picked_refs = source_refs[-(origins_ref.shape[0] // semaphores.shape[1]) :]
    source_refs = source_refs[: semaphores.shape[1]]
    copies = []
    for k, picked_ref in enumerate(picked_refs):
        for j, source_ref in enumerate(source_refs):
            origin = pl.multiple_of(origins_ref[k * len(source_refs) + j], picked_ref.shape[2])
            columns = source_ref.at[:, pl.ds(origin, picked_ref.shape[2])]
            copies.append(pltpu.make_async_copy(columns, picked_ref.at[j], semaphores.at[k, j]))
            copies[-1].start()
    for copy in copies:
        copy.wait()


def pick_columns(sources, origins, *shapes):
    return pl.pallas_call(
        pick_kernel,
        out_shape=shapes,
        in_specs=[pl.BlockSpec(memory_space=pltpu.SMEM)] + [pl.BlockSpec(memory_space=pl.ANY)] * len(sources),
        out_specs=[pl.BlockSpec(memory_space=pl.ANY)] * len(shapes),
        scratch_shapes=[pltpu.SemaphoreType.DMA((len(shapes), len(sources)))],
        compiler_params=pltpu.CompilerParams(vmem_limit_bytes=1 << 20),
        name="pick",
    )(jnp.stack(origins).astype(jnp.int32), in_hbm(sources[0]), *sources[1:])


def spread_kernel(relayed_ref, blocks_ref):
    images, tokens, features = relayed_ref.shape
    block = relayed_ref[...].astype(jnp.float32).reshape(images * tokens, features).T.astype(jnp.bfloat16)
    for k in range(blocks_ref.shape[0]):
        blocks_ref[k] = block


def turn_kernel(column_ref, turned_ref):
    turned_ref[...] = column_ref[...].astype(jnp.float32).T.astype(jnp.bfloat16)


def project_kernel(member_ref, group_ref, *refs):
    *chunk_refs, part_ref = refs
    part = jnp.zeros(part_ref.shape, jnp.float32)
    for across_y, chunk_ref in enumerate(chunk_refs):
        for across_x in range(chunk_ref.shape[0]):
            there = member_ref[0] ^ (2 * across_y + across_x)
            part += jnp.dot(group_ref[there], chunk_ref[across_x], preferred_element_type=jnp.float32)
    part_ref[...] = part.astype(jnp.bfloat16)


def finish_kernel(parts_ref, residual_ref, mixed_ref):
    row_0, row_1, col_0, col_1, _, width = parts_ref.shape
    for r in range(row_1):
        for c in range(col_1):
            here = pl.ds((c * row_1 + r) * width, width)
            total = residual_ref[:, here]
            for i in range(row_0):
                for j in range(col_0):
                    total += parts_ref[i, r, j, c].astype(jnp.float32)
            mixed_ref[:, here] = total.astype(jnp.bfloat16)


def attend(visual, vis_gain, text, text_gain, query_weight, key_weight, value_weight, out_weight):
    rows, cols, quad = (lax.axis_size(a) for a in (ROW, COL, QUAD))
    images = lax.axis_size("dp")
    devices = rows * cols
    tokens, _, features = visual.shape
    text_tokens = text.shape[0]
    tokens_here = text_tokens // devices
    width = DEC // quad
    member = lax.axis_index(QUAD)
    relayed = visual.transpose(1, 0, 2)
    relayed = lax.all_to_all(relayed, "dp", 0, 0, tiled=True)
    row, col = (lax.axis_index(a) for a in QUAD)
    swap = [(0, 1), (1, 0)]
    half = DEC // 2
    quarter = jax.ShapeDtypeStruct((2, HEAD_DIM, width), jnp.bfloat16)
    send = pick_columns([out_weight], [(1 - col) * half], jax.ShapeDtypeStruct((1, HEAD_DIM, half), jnp.bfloat16))[0]
    beyond = lax.ppermute(send, QUAD[1], swap)[0]
    origins = [[col * half + r * width, r * width] for r in (row, 1 - row)]
    keep, send = pick_columns([out_weight, beyond], origins[0] + origins[1], quarter, quarter)
    out_rows = [keep, lax.ppermute(send, QUAD[0], swap)]
    vis_tokens = images * tokens
    blocks = pl.pallas_call(
        spread_kernel,
        out_shape=jax.ShapeDtypeStruct((rows, features, vis_tokens), jnp.bfloat16),
        in_specs=[pl.BlockSpec(memory_space=pltpu.VMEM)],
        out_specs=pl.BlockSpec(memory_space=pltpu.VMEM),
        compiler_params=pltpu.CompilerParams(vmem_limit_bytes=4 << 20),
        name="spread",
    )(in_vmem(relayed))
    column = lax.all_to_all(blocks, ROW, 0, 0, tiled=True)
    flat = text.reshape(text_tokens, DEC)
    queries, residual = pl.pallas_call(
        query_kernel,
        out_shape=(
            jax.ShapeDtypeStruct((text_tokens, HEAD_DIM), jnp.bfloat16),
            jax.ShapeDtypeStruct((tokens_here, DEC), jnp.float32),
        ),
        in_specs=[pl.BlockSpec(memory_space=pltpu.SMEM)]
        + [pl.BlockSpec(memory_space=pl.ANY)] * 2
        + [pl.BlockSpec(memory_space=pltpu.VMEM)],
        out_specs=[pl.BlockSpec(memory_space=pltpu.VMEM)] * 2,
        scratch_shapes=[
            pltpu.VMEM(flat.shape, jnp.bfloat16),
            pltpu.VMEM(query_weight.shape, jnp.bfloat16),
            pltpu.VMEM((text_tokens // TEXT_CHUNKS, DEC), jnp.bfloat16),
            pltpu.SemaphoreType.DMA((TEXT_CHUNKS + 1,)),
        ],
        compiler_params=pltpu.CompilerParams(vmem_limit_bytes=8 << 20),
        name="query",
    )(
        (lax.axis_index(MP) * tokens_here).reshape(1),
        in_hbm(flat),
        in_hbm(query_weight),
        text_gain.reshape(1, DEC),
    )
    gain = vis_gain.reshape(rows, cols, features).transpose(1, 0, 2).reshape(cols, rows * features)
    column = pl.pallas_call(
        turn_kernel,
        out_shape=jax.ShapeDtypeStruct((vis_tokens, rows * features), jnp.bfloat16),
        in_specs=[pl.BlockSpec(memory_space=pltpu.VMEM)],
        out_specs=pl.BlockSpec(memory_space=pltpu.VMEM),
        compiler_params=pltpu.CompilerParams(vmem_limit_bytes=4 << 20),
        name="turn",
    )(in_vmem(column.reshape(rows * features, vis_tokens)))
    column = (column.astype(jnp.float32) * SCALE).astype(jnp.float16)
    whole = lax.all_gather(column, COL, axis=0, tiled=True)
    whole = whole.astype(jnp.bfloat16).reshape(cols, vis_tokens, rows * features)
    operands = [in_vmem(v) for v in (whole, gain, queries)]
    operands += [in_hbm(w.reshape(rows, cols, features, HEAD_DIM)) for w in (key_weight, value_weight)]
    contexts = pl.pallas_call(
        attention_kernel,
        out_shape=jax.ShapeDtypeStruct((quad, text_tokens, HEAD_DIM), jnp.bfloat16),
        in_specs=[pl.BlockSpec(memory_space=pltpu.VMEM)] * 3 + [pl.BlockSpec(memory_space=pltpu.HBM)] * 2,
        out_specs=pl.BlockSpec(memory_space=pltpu.VMEM),
        scratch_shapes=[
            *(pltpu.VMEM(w.shape, jnp.bfloat16) for w in operands[3:]),
            pltpu.SemaphoreType.DMA((2, cols)),
            pltpu.VMEM(whole.shape, jnp.bfloat16),
            *[pltpu.VMEM((vis_tokens, LANES), jnp.float32)] * 2,
        ],
        compiler_params=pltpu.CompilerParams(vmem_limit_bytes=12 << 20),
        name="attention",
    )(*operands)
    group = lax.all_to_all(contexts, QUAD, 0, 0, tiled=True)
    operands = [in_vmem(v) for v in (group, *out_rows)]
    part = pl.pallas_call(
        project_kernel,
        out_shape=jax.ShapeDtypeStruct((text_tokens, width), jnp.bfloat16),
        in_specs=[pl.BlockSpec(memory_space=pltpu.SMEM)] + [pl.BlockSpec(memory_space=pltpu.VMEM)] * len(operands),
        out_specs=pl.BlockSpec(memory_space=pltpu.VMEM),
        compiler_params=pltpu.CompilerParams(vmem_limit_bytes=12 << 20),
        name="project",
    )(member.reshape(1), *operands)
    parts = lax.all_to_all(part.reshape(devices, tokens_here, width), MP, 0, 0, tiled=True)
    parts = parts.reshape(*(lax.axis_size(a) for a in MP), tokens_here, width)
    mixed = pl.pallas_call(
        finish_kernel,
        out_shape=jax.ShapeDtypeStruct((tokens_here, DEC), jnp.bfloat16),
        in_specs=[pl.BlockSpec(memory_space=pltpu.VMEM)] * 2,
        out_specs=pl.BlockSpec(memory_space=pltpu.VMEM),
        compiler_params=pltpu.CompilerParams(vmem_limit_bytes=12 << 20),
        name="finish",
    )(in_vmem(parts), in_vmem(residual))
    return mixed.reshape(tokens_here, 1, DEC)


def solution(mesh):
    split = Mesh(mesh.devices.reshape(mesh.shape["dp"], 2, 2, 4, 2), ("dp",) + MP)
    in_specs = (
        P("dp", None, MP),
        P(),
        P(None, "dp", None),
        P(),
        P(None, MP),
        P(None, MP),
        P(None, MP),
        P(MP, None),
    )
    out_specs = P(MP, "dp", None)
    return jax.shard_map(attend, mesh=split, in_specs=in_specs, out_specs=out_specs, check_vma=False)
```

```python
import jax
import jax.numpy as jnp
from jax import lax
from jax.experimental import pallas as pl
from jax.experimental.pallas import tpu as pltpu
from jax.sharding import Mesh
from jax.sharding import PartitionSpec as P


DEC = 4096
HEAD_DIM = 128
DP = ("dp_0", "dp_1")
ROW = ("row_0", "row_1")
COL = ("col_0", "col_1")
MP = ROW + COL
QUAD = ("row_1", "col_1")
LANES = 128
CHUNK = 128
TEXT_CHUNKS = 2
TEXT_BLOCK = 32
SCALE = 8192.0

epsilon = 1e-06


def in_vmem(value):
    return pltpu.with_memory_space_constraint(value, pltpu.VMEM)


def in_hbm(value):
    return pltpu.with_memory_space_constraint(value, pltpu.HBM)


def attention_kernel(
    whole_ref,
    gain_ref,
    queries_ref,
    key_hbm_ref,
    value_hbm_ref,
    contexts_ref,
    key_ref,
    value_ref,
    semaphores,
    normed_ref,
    scale_ref,
):
    key_copy = pltpu.make_async_copy(key_hbm_ref, key_ref, semaphores.at[0])
    value_copy = pltpu.make_async_copy(value_hbm_ref, value_ref, semaphores.at[1])
    key_copy.start()
    value_copy.start()
    cols, tokens, depth = whole_ref.shape
    rows = key_ref.shape[0] // cols
    count = cols * depth
    places = [(c, pl.ds(k, LANES)) for c in range(cols) for k in range(0, depth, LANES)]

    def normalize(step, carry):
        here = pl.ds(pl.multiple_of(step * CHUNK, CHUNK), CHUNK)
        sums = jnp.zeros((CHUNK, LANES), jnp.float32)
        for c, k in places:
            sums += whole_ref[c, here, k].astype(jnp.float32)
        mean = jnp.sum(sums, axis=1, keepdims=True) / count
        squares = jnp.zeros((CHUNK, LANES), jnp.float32)
        for c, k in places:
            centred = whole_ref[c, here, k].astype(jnp.float32) - mean
            squares += centred * centred
            normed_ref[c, here, k] = (centred * gain_ref[c : c + 1, k]).astype(jnp.bfloat16)
        spread = jnp.sum(squares, axis=1, keepdims=True) / count
        scale_ref[here, :] = jnp.broadcast_to(lax.rsqrt(spread + epsilon * SCALE * SCALE), (CHUNK, LANES))
        return carry

    lax.fori_loop(0, tokens // CHUNK, normalize, 0)
    key_copy.wait()
    value_copy.wait()
    projected = jnp.zeros((tokens, 2 * HEAD_DIM), jnp.float32)
    for c in range(cols):
        both = [jnp.concatenate([ref[r * cols + c] for r in range(rows)], axis=0) for ref in (key_ref, value_ref)]
        projected += jnp.dot(normed_ref[c], jnp.concatenate(both, axis=1), preferred_element_type=jnp.float32)
    keys = (projected[:, :HEAD_DIM] * scale_ref[...]).astype(jnp.bfloat16)
    values = (projected[:, HEAD_DIM:] * scale_ref[...]).astype(jnp.bfloat16)
    scores = lax.dot_general(queries_ref[...], keys, (((1,), (1,)), ((), ())), preferred_element_type=jnp.float32)
    scores *= HEAD_DIM**-0.5
    weights = jnp.exp(scores - jnp.max(scores, axis=1, keepdims=True))
    probs = (weights / jnp.sum(weights, axis=1, keepdims=True)).astype(jnp.bfloat16)
    context = jnp.dot(probs, values, preferred_element_type=jnp.float32).astype(jnp.bfloat16)
    for k in range(contexts_ref.shape[0]):
        contexts_ref[k] = context


def query_kernel(
    origin_ref,
    text_hbm_ref,
    weight_hbm_ref,
    gain_ref,
    queries_ref,
    residual_ref,
    text_ref,
    weight_ref,
    normed_ref,
    semaphores,
):
    tokens, width = text_ref.shape
    chunk = tokens // TEXT_CHUNKS
    places = [pl.ds(k * chunk, chunk) for k in range(TEXT_CHUNKS)]
    copies = [
        pltpu.make_async_copy(text_hbm_ref.at[here], text_ref.at[here], semaphores.at[k])
        for k, here in enumerate(places)
    ]
    copies.append(pltpu.make_async_copy(weight_hbm_ref, weight_ref, semaphores.at[TEXT_CHUNKS]))
    for copy in copies:
        copy.start()
    for k, here in enumerate(places):
        copies[k].wait()

        def normalize(step, carry, k=k):
            block = pl.ds(pl.multiple_of(step * TEXT_BLOCK, TEXT_BLOCK), TEXT_BLOCK)
            inside = pl.ds(pl.multiple_of(k * chunk + step * TEXT_BLOCK, TEXT_BLOCK), TEXT_BLOCK)
            squares = jnp.zeros((TEXT_BLOCK, LANES), jnp.float32)
            for n in range(0, width, LANES):
                x = text_ref[inside, pl.ds(n, LANES)].astype(jnp.float32)
                squares += x * x
            scale = lax.rsqrt(jnp.sum(squares, axis=1, keepdims=True) / width + epsilon)
            for n in range(0, width, LANES):
                x = text_ref[inside, pl.ds(n, LANES)].astype(jnp.float32)
                normed_ref[block, pl.ds(n, LANES)] = (x * scale * gain_ref[:, pl.ds(n, LANES)]).astype(jnp.bfloat16)
            return carry

        lax.fori_loop(0, chunk // TEXT_BLOCK, normalize, 0)
        if k == 0:
            copies[-1].wait()
        queries_ref[here, :] = jnp.dot(
            normed_ref[...], weight_ref[...], preferred_element_type=jnp.float32
        ).astype(jnp.bfloat16)
    count = residual_ref.shape[0]
    pair = text_ref[pl.ds(pl.multiple_of(origin_ref[0] // 16 * 16, 16), 16), :].astype(jnp.float32)
    residual_ref[...] = jnp.where(origin_ref[0] % 16 == 0, pair[:count], pair[count:])


def pick_kernel(origins_ref, *refs):
    *source_refs, semaphores = refs
    picked_refs = source_refs[-(origins_ref.shape[0] // semaphores.shape[1]) :]
    source_refs = source_refs[: semaphores.shape[1]]
    copies = []
    for k, picked_ref in enumerate(picked_refs):
        for j, source_ref in enumerate(source_refs):
            origin = pl.multiple_of(origins_ref[k * len(source_refs) + j], picked_ref.shape[2])
            columns = source_ref.at[:, pl.ds(origin, picked_ref.shape[2])]
            copies.append(pltpu.make_async_copy(columns, picked_ref.at[j], semaphores.at[k, j]))
            copies[-1].start()
    for copy in copies:
        copy.wait()


def pick_columns(sources, origins, *shapes):
    return pl.pallas_call(
        pick_kernel,
        out_shape=shapes,
        in_specs=[pl.BlockSpec(memory_space=pltpu.SMEM)] + [pl.BlockSpec(memory_space=pl.ANY)] * len(sources),
        out_specs=[pl.BlockSpec(memory_space=pl.ANY)] * len(shapes),
        scratch_shapes=[pltpu.SemaphoreType.DMA((len(shapes), len(sources)))],
        compiler_params=pltpu.CompilerParams(vmem_limit_bytes=1 << 20),
        name="pick",
    )(jnp.stack(origins).astype(jnp.int32), in_hbm(sources[0]), *sources[1:])


def deal_kernel(visual_ref, dealt_ref):
    planes, halves = dealt_ref.shape[:2]
    dealt = jnp.swapaxes(visual_ref[...].astype(jnp.float32), 0, 1).astype(jnp.bfloat16)
    for h in range(halves):
        for p in range(planes):
            dealt_ref[p, h] = dealt[h * planes + p]


def spread_kernel(relayed_ref, blocks_ref):
    planes, halves, tokens, features = relayed_ref.shape
    copies = blocks_ref.shape[0] // halves
    for h in range(halves):
        block = relayed_ref[:, h].astype(jnp.float32).reshape(planes * tokens, features).T.astype(jnp.bfloat16)
        for k in range(copies):
            blocks_ref[h * copies + k] = block


def turn_kernel(column_ref, turned_ref):
    halves, _, half_tokens = column_ref.shape
    for h in range(halves):
        turned = column_ref[h].astype(jnp.float32).T
        turned_ref[pl.ds(h * half_tokens, half_tokens), :] = turned.astype(jnp.bfloat16)


def project_kernel(member_ref, group_ref, *refs):
    *chunk_refs, part_ref = refs
    part = jnp.zeros(part_ref.shape, jnp.float32)
    for across_y, chunk_ref in enumerate(chunk_refs):
        for across_x in range(chunk_ref.shape[0]):
            there = member_ref[0] ^ (2 * across_y + across_x)
            part += jnp.dot(group_ref[there], chunk_ref[across_x], preferred_element_type=jnp.float32)
    part_ref[...] = part.astype(jnp.bfloat16)


def finish_kernel(parts_ref, residual_ref, mixed_ref):
    row_0, row_1, col_0, col_1, _, width = parts_ref.shape
    for r in range(row_1):
        for c in range(col_1):
            here = pl.ds((c * row_1 + r) * width, width)
            total = residual_ref[:, here]
            for i in range(row_0):
                for j in range(col_0):
                    total += parts_ref[i, r, j, c].astype(jnp.float32)
            mixed_ref[:, here] = total.astype(jnp.bfloat16)


def attend(visual, vis_gain, text, text_gain, query_weight, key_weight, value_weight, out_weight):
    rows, cols, quad = (lax.axis_size(a) for a in (ROW, COL, QUAD))
    halves, planes = (lax.axis_size(a) for a in DP)
    devices = rows * cols
    tokens, _, features = visual.shape
    text_tokens = text.shape[0]
    tokens_here = text_tokens // devices
    width = DEC // quad
    member = lax.axis_index(QUAD)
    relayed = pl.pallas_call(
        deal_kernel,
        out_shape=jax.ShapeDtypeStruct((planes, halves, tokens, features), jnp.bfloat16),
        in_specs=[pl.BlockSpec(memory_space=pltpu.VMEM)],
        out_specs=pl.BlockSpec(memory_space=pltpu.VMEM),
        compiler_params=pltpu.CompilerParams(vmem_limit_bytes=4 << 20),
        name="deal",
    )(visual)
    relayed = lax.all_to_all(relayed, "dp_1", 0, 0, tiled=True)
    row, col = (lax.axis_index(a) for a in QUAD)
    swap = [(0, 1), (1, 0)]
    half = DEC // 2
    quarter = jax.ShapeDtypeStruct((2, HEAD_DIM, width), jnp.bfloat16)
    send = pick_columns([out_weight], [(1 - col) * half], jax.ShapeDtypeStruct((1, HEAD_DIM, half), jnp.bfloat16))[0]
    beyond = lax.ppermute(send, QUAD[1], swap)[0]
    origins = [[col * half + r * width, r * width] for r in (row, 1 - row)]
    keep, send = pick_columns([out_weight, beyond], origins[0] + origins[1], quarter, quarter)
    out_rows = [keep, lax.ppermute(send, QUAD[0], swap)]
    half_tokens = planes * tokens
    blocks = pl.pallas_call(
        spread_kernel,
        out_shape=jax.ShapeDtypeStruct((halves * rows, features, half_tokens), jnp.bfloat16),
        in_specs=[pl.BlockSpec(memory_space=pltpu.VMEM)],
        out_specs=pl.BlockSpec(memory_space=pltpu.VMEM),
        compiler_params=pltpu.CompilerParams(vmem_limit_bytes=4 << 20),
        name="spread",
    )(in_vmem(relayed))
    column = lax.all_to_all(blocks, ("dp_0",) + ROW, 0, 0, tiled=True)
    flat = text.reshape(text_tokens, DEC)
    queries, residual = pl.pallas_call(
        query_kernel,
        out_shape=(
            jax.ShapeDtypeStruct((text_tokens, HEAD_DIM), jnp.bfloat16),
            jax.ShapeDtypeStruct((tokens_here, DEC), jnp.float32),
        ),
        in_specs=[pl.BlockSpec(memory_space=pltpu.SMEM)]
        + [pl.BlockSpec(memory_space=pl.ANY)] * 2
        + [pl.BlockSpec(memory_space=pltpu.VMEM)],
        out_specs=[pl.BlockSpec(memory_space=pltpu.VMEM)] * 2,
        scratch_shapes=[
            pltpu.VMEM(flat.shape, jnp.bfloat16),
            pltpu.VMEM(query_weight.shape, jnp.bfloat16),
            pltpu.VMEM((text_tokens // TEXT_CHUNKS, DEC), jnp.bfloat16),
            pltpu.SemaphoreType.DMA((TEXT_CHUNKS + 1,)),
        ],
        compiler_params=pltpu.CompilerParams(vmem_limit_bytes=8 << 20),
        name="query",
    )(
        (lax.axis_index(MP) * tokens_here).reshape(1),
        in_hbm(flat),
        in_hbm(query_weight),
        text_gain.reshape(1, DEC),
    )
    gain = vis_gain.reshape(rows, cols, features).transpose(1, 0, 2).reshape(cols, rows * features)
    column = pl.pallas_call(
        turn_kernel,
        out_shape=jax.ShapeDtypeStruct((halves * half_tokens, rows * features), jnp.bfloat16),
        in_specs=[pl.BlockSpec(memory_space=pltpu.VMEM)],
        out_specs=pl.BlockSpec(memory_space=pltpu.VMEM),
        compiler_params=pltpu.CompilerParams(vmem_limit_bytes=4 << 20),
        name="turn",
    )(in_vmem(column.reshape(halves, rows * features, half_tokens)))
    column = (column.astype(jnp.float32) * SCALE).astype(jnp.float16)
    whole = lax.all_gather(column, COL, axis=0, tiled=True)
    whole = whole.astype(jnp.bfloat16).reshape(cols, halves * half_tokens, rows * features)
    operands = [in_vmem(v) for v in (whole, gain, queries)]
    operands += [in_hbm(w.reshape(devices, features, HEAD_DIM)) for w in (key_weight, value_weight)]
    contexts = pl.pallas_call(
        attention_kernel,
        out_shape=jax.ShapeDtypeStruct((quad, text_tokens, HEAD_DIM), jnp.bfloat16),
        in_specs=[pl.BlockSpec(memory_space=pltpu.VMEM)] * 3 + [pl.BlockSpec(memory_space=pltpu.HBM)] * 2,
        out_specs=pl.BlockSpec(memory_space=pltpu.VMEM),
        scratch_shapes=[
            *(pltpu.VMEM(w.shape, jnp.bfloat16) for w in operands[3:]),
            pltpu.SemaphoreType.DMA((2,)),
            pltpu.VMEM(whole.shape, jnp.bfloat16),
            pltpu.VMEM((whole.shape[1], LANES), jnp.float32),
        ],
        compiler_params=pltpu.CompilerParams(vmem_limit_bytes=12 << 20),
        name="attention",
    )(*operands)
    contexts, member, *out_rows = lax.optimization_barrier((contexts, member.reshape(1), *out_rows))
    group = lax.all_to_all(contexts, QUAD, 0, 0, tiled=True)
    operands = [in_vmem(v) for v in (group, *out_rows)]
    part = pl.pallas_call(
        project_kernel,
        out_shape=jax.ShapeDtypeStruct((text_tokens, width), jnp.bfloat16),
        in_specs=[pl.BlockSpec(memory_space=pltpu.SMEM)] + [pl.BlockSpec(memory_space=pltpu.VMEM)] * len(operands),
        out_specs=pl.BlockSpec(memory_space=pltpu.VMEM),
        compiler_params=pltpu.CompilerParams(vmem_limit_bytes=12 << 20),
        name="project",
    )(member, *operands)
    parts = lax.all_to_all(part.reshape(devices, tokens_here, width), MP, 0, 0, tiled=True)
    parts = parts.reshape(*(lax.axis_size(a) for a in MP), tokens_here, width)
    mixed = pl.pallas_call(
        finish_kernel,
        out_shape=jax.ShapeDtypeStruct((tokens_here, DEC), jnp.bfloat16),
        in_specs=[pl.BlockSpec(memory_space=pltpu.VMEM)] * 2,
        out_specs=pl.BlockSpec(memory_space=pltpu.VMEM),
        compiler_params=pltpu.CompilerParams(vmem_limit_bytes=12 << 20),
        name="finish",
    )(in_vmem(parts), in_vmem(residual))
    return mixed.reshape(tokens_here, 1, DEC)


def solution(mesh):
    split = Mesh(mesh.devices.reshape(2, mesh.shape["dp"] // 2, 2, 2, 4, 2), DP + MP)
    in_specs = (
        P(DP, None, MP),
        P(),
        P(None, DP, None),
        P(),
        P(None, MP),
        P(None, MP),
        P(None, MP),
        P(MP, None),
    )
    out_specs = P(MP, DP, None)
    return jax.shard_map(attend, mesh=split, in_specs=in_specs, out_specs=out_specs, check_vma=False)
```

```python
import jax
import jax.numpy as jnp
from jax import lax
from jax.experimental import pallas as pl
from jax.experimental.pallas import tpu as pltpu
from jax.sharding import Mesh
from jax.sharding import PartitionSpec as P


DEC = 4096
HEAD_DIM = 128
DP = ("dp_0", "dp_1")
ROW = ("row_0", "row_1")
COL = ("col_0", "col_1")
MP = ROW + COL
QUAD = ("row_1", "col_1")
LANES = 128
CHUNK = 128
TEXT_CHUNKS = 2
TEXT_BLOCK = 32
SCALE = 8192.0

epsilon = 1e-06


def in_vmem(value):
    return pltpu.with_memory_space_constraint(value, pltpu.VMEM)


def in_hbm(value):
    return pltpu.with_memory_space_constraint(value, pltpu.HBM)


def attention_kernel(
    whole_ref,
    gain_ref,
    queries_ref,
    key_hbm_ref,
    value_hbm_ref,
    contexts_ref,
    key_ref,
    value_ref,
    semaphores,
    normed_ref,
    scale_ref,
):
    key_copy = pltpu.make_async_copy(key_hbm_ref, key_ref, semaphores.at[0])
    value_copy = pltpu.make_async_copy(value_hbm_ref, value_ref, semaphores.at[1])
    key_copy.start()
    value_copy.start()
    cols, tokens, depth = whole_ref.shape
    rows = key_ref.shape[0] // cols
    count = cols * depth
    places = [(c, pl.ds(k, LANES)) for c in range(cols) for k in range(0, depth, LANES)]

    def normalize(step, carry):
        here = pl.ds(pl.multiple_of(step * CHUNK, CHUNK), CHUNK)
        sums = jnp.zeros((CHUNK, LANES), jnp.float32)
        for c, k in places:
            sums += whole_ref[c, here, k].astype(jnp.float32)
        mean = jnp.sum(sums, axis=1, keepdims=True) / count
        squares = jnp.zeros((CHUNK, LANES), jnp.float32)
        for c, k in places:
            centred = whole_ref[c, here, k].astype(jnp.float32) - mean
            squares += centred * centred
            normed_ref[c, here, k] = (centred * gain_ref[c : c + 1, k]).astype(jnp.bfloat16)
        spread = jnp.sum(squares, axis=1, keepdims=True) / count
        scale_ref[here, :] = jnp.broadcast_to(lax.rsqrt(spread + epsilon * SCALE * SCALE), (CHUNK, LANES))
        return carry

    lax.fori_loop(0, tokens // CHUNK, normalize, 0)
    key_copy.wait()
    value_copy.wait()
    projected = jnp.zeros((tokens, 2 * HEAD_DIM), jnp.float32)
    for c in range(cols):
        both = [jnp.concatenate([ref[r * cols + c] for r in range(rows)], axis=0) for ref in (key_ref, value_ref)]
        projected += jnp.dot(normed_ref[c], jnp.concatenate(both, axis=1), preferred_element_type=jnp.float32)
    keys = (projected[:, :HEAD_DIM] * scale_ref[...]).astype(jnp.bfloat16)
    values = (projected[:, HEAD_DIM:] * scale_ref[...]).astype(jnp.bfloat16)
    scores = lax.dot_general(queries_ref[...], keys, (((1,), (1,)), ((), ())), preferred_element_type=jnp.float32)
    scores *= HEAD_DIM**-0.5
    weights = jnp.exp(scores - jnp.max(scores, axis=1, keepdims=True))
    probs = (weights / jnp.sum(weights, axis=1, keepdims=True)).astype(jnp.bfloat16)
    context = jnp.dot(probs, values, preferred_element_type=jnp.float32).astype(jnp.bfloat16)
    for k in range(contexts_ref.shape[0]):
        contexts_ref[k] = context


def query_kernel(
    origin_ref,
    text_hbm_ref,
    weight_hbm_ref,
    gain_ref,
    queries_ref,
    residual_ref,
    text_ref,
    weight_ref,
    normed_ref,
    semaphores,
):
    tokens, width = text_ref.shape
    chunk = tokens // TEXT_CHUNKS
    places = [pl.ds(k * chunk, chunk) for k in range(TEXT_CHUNKS)]
    copies = [
        pltpu.make_async_copy(text_hbm_ref.at[here], text_ref.at[here], semaphores.at[k])
        for k, here in enumerate(places)
    ]
    copies.append(pltpu.make_async_copy(weight_hbm_ref, weight_ref, semaphores.at[TEXT_CHUNKS]))
    for copy in copies:
        copy.start()
    for k, here in enumerate(places):
        copies[k].wait()

        def normalize(step, carry, k=k):
            block = pl.ds(pl.multiple_of(step * TEXT_BLOCK, TEXT_BLOCK), TEXT_BLOCK)
            inside = pl.ds(pl.multiple_of(k * chunk + step * TEXT_BLOCK, TEXT_BLOCK), TEXT_BLOCK)
            squares = jnp.zeros((TEXT_BLOCK, LANES), jnp.float32)
            for n in range(0, width, LANES):
                x = text_ref[inside, pl.ds(n, LANES)].astype(jnp.float32)
                squares += x * x
            scale = lax.rsqrt(jnp.sum(squares, axis=1, keepdims=True) / width + epsilon)
            for n in range(0, width, LANES):
                x = text_ref[inside, pl.ds(n, LANES)].astype(jnp.float32)
                normed_ref[block, pl.ds(n, LANES)] = (x * scale * gain_ref[:, pl.ds(n, LANES)]).astype(jnp.bfloat16)
            return carry

        lax.fori_loop(0, chunk // TEXT_BLOCK, normalize, 0)
        if k == 0:
            copies[-1].wait()
        queries_ref[here, :] = jnp.dot(
            normed_ref[...], weight_ref[...], preferred_element_type=jnp.float32
        ).astype(jnp.bfloat16)
    count = residual_ref.shape[0]
    pair = text_ref[pl.ds(pl.multiple_of(origin_ref[0] // 16 * 16, 16), 16), :].astype(jnp.float32)
    residual_ref[...] = jnp.where(origin_ref[0] % 16 == 0, pair[:count], pair[count:])


def pick_kernel(origins_ref, *refs):
    *source_refs, semaphores = refs
    picked_refs = source_refs[-(origins_ref.shape[0] // semaphores.shape[1]) :]
    source_refs = source_refs[: semaphores.shape[1]]
    copies = []
    for k, picked_ref in enumerate(picked_refs):
        for j, source_ref in enumerate(source_refs):
            origin = pl.multiple_of(origins_ref[k * len(source_refs) + j], picked_ref.shape[2])
            columns = source_ref.at[:, pl.ds(origin, picked_ref.shape[2])]
            copies.append(pltpu.make_async_copy(columns, picked_ref.at[j], semaphores.at[k, j]))
            copies[-1].start()
    for copy in copies:
        copy.wait()


def pick_columns(sources, origins, *shapes):
    return pl.pallas_call(
        pick_kernel,
        out_shape=shapes,
        in_specs=[pl.BlockSpec(memory_space=pltpu.SMEM)] + [pl.BlockSpec(memory_space=pl.ANY)] * len(sources),
        out_specs=[pl.BlockSpec(memory_space=pl.ANY)] * len(shapes),
        scratch_shapes=[pltpu.SemaphoreType.DMA((len(shapes), len(sources)))],
        compiler_params=pltpu.CompilerParams(vmem_limit_bytes=1 << 20),
        name="pick",
    )(jnp.stack(origins).astype(jnp.int32), in_hbm(sources[0]), *sources[1:])


def deal_kernel(visual_hbm_ref, dealt_hbm_ref, visual_ref, dealt_ref, semaphores):
    planes, halves = dealt_hbm_ref.shape[:2]
    loads, stores = [], []
    for h in range(halves):
        here = pl.ds(h * planes, planes)
        loads.append(pltpu.make_async_copy(visual_hbm_ref.at[:, here], visual_ref.at[:, here], semaphores.at[0, h]))
        stores.append(pltpu.make_async_copy(dealt_ref.at[h], dealt_hbm_ref.at[:, h], semaphores.at[1, h]))
        loads[h].start()
    for h in range(halves):
        loads[h].wait()
        half = visual_ref[:, pl.ds(h * planes, planes)].astype(jnp.float32)
        dealt_ref[h] = jnp.swapaxes(half, 0, 1).astype(jnp.bfloat16)
        stores[h].start()
    for store in stores:
        store.wait()


def spread_kernel(relayed_ref, blocks_ref):
    planes, halves, tokens, features = relayed_ref.shape
    copies = blocks_ref.shape[0] // halves
    for h in range(halves):
        block = relayed_ref[:, h].astype(jnp.float32).reshape(planes * tokens, features).T.astype(jnp.bfloat16)
        for k in range(copies):
            blocks_ref[h * copies + k] = block


def turn_kernel(column_ref, turned_ref):
    halves, _, half_tokens = column_ref.shape
    for h in range(halves):
        turned = column_ref[h].astype(jnp.float32).T
        turned_ref[pl.ds(h * half_tokens, half_tokens), :] = turned.astype(jnp.bfloat16)


def project_kernel(member_ref, group_ref, *refs):
    *chunk_refs, part_ref = refs
    part = jnp.zeros(part_ref.shape, jnp.float32)
    for across_y, chunk_ref in enumerate(chunk_refs):
        for across_x in range(chunk_ref.shape[0]):
            there = member_ref[0] ^ (2 * across_y + across_x)
            part += jnp.dot(group_ref[there], chunk_ref[across_x], preferred_element_type=jnp.float32)
    part_ref[...] = part.astype(jnp.bfloat16)


def finish_kernel(parts_ref, residual_ref, mixed_ref):
    row_0, row_1, col_0, col_1, _, width = parts_ref.shape
    for r in range(row_1):
        for c in range(col_1):
            here = pl.ds((c * row_1 + r) * width, width)
            total = residual_ref[:, here]
            for i in range(row_0):
                for j in range(col_0):
                    total += parts_ref[i, r, j, c].astype(jnp.float32)
            mixed_ref[:, here] = total.astype(jnp.bfloat16)


def attend(visual, vis_gain, text, text_gain, query_weight, key_weight, value_weight, out_weight):
    rows, cols, quad = (lax.axis_size(a) for a in (ROW, COL, QUAD))
    halves, planes = (lax.axis_size(a) for a in DP)
    devices = rows * cols
    tokens, _, features = visual.shape
    text_tokens = text.shape[0]
    tokens_here = text_tokens // devices
    width = DEC // quad
    member = lax.axis_index(QUAD)
    relayed = pl.pallas_call(
        deal_kernel,
        out_shape=jax.ShapeDtypeStruct((planes, halves, tokens, features), jnp.bfloat16),
        in_specs=[pl.BlockSpec(memory_space=pl.ANY)],
        out_specs=pl.BlockSpec(memory_space=pl.ANY),
        scratch_shapes=[
            pltpu.VMEM(visual.shape, jnp.bfloat16),
            pltpu.VMEM((halves, planes, tokens, features), jnp.bfloat16),
            pltpu.SemaphoreType.DMA((2, halves)),
        ],
        compiler_params=pltpu.CompilerParams(vmem_limit_bytes=4 << 20),
        name="deal",
    )(in_hbm(visual))
    relayed = lax.all_to_all(relayed, "dp_1", 0, 0, tiled=True)
    row, col = (lax.axis_index(a) for a in QUAD)
    swap = [(0, 1), (1, 0)]
    half = DEC // 2
    quarter = jax.ShapeDtypeStruct((2, HEAD_DIM, width), jnp.bfloat16)
    send = pick_columns([out_weight], [(1 - col) * half], jax.ShapeDtypeStruct((1, HEAD_DIM, half), jnp.bfloat16))[0]
    beyond = lax.ppermute(send, QUAD[1], swap)[0]
    origins = [[col * half + r * width, r * width] for r in (row, 1 - row)]
    keep, send = pick_columns([out_weight, beyond], origins[0] + origins[1], quarter, quarter)
    out_rows = [keep, lax.ppermute(send, QUAD[0], swap)]
    half_tokens = planes * tokens
    blocks = pl.pallas_call(
        spread_kernel,
        out_shape=jax.ShapeDtypeStruct((halves * rows, features, half_tokens), jnp.bfloat16),
        in_specs=[pl.BlockSpec(memory_space=pltpu.VMEM)],
        out_specs=pl.BlockSpec(memory_space=pltpu.VMEM),
        compiler_params=pltpu.CompilerParams(vmem_limit_bytes=4 << 20),
        name="spread",
    )(in_vmem(relayed))
    column = lax.all_to_all(blocks, ("dp_0",) + ROW, 0, 0, tiled=True)
    flat = text.reshape(text_tokens, DEC)
    queries, residual = pl.pallas_call(
        query_kernel,
        out_shape=(
            jax.ShapeDtypeStruct((text_tokens, HEAD_DIM), jnp.bfloat16),
            jax.ShapeDtypeStruct((tokens_here, DEC), jnp.float32),
        ),
        in_specs=[pl.BlockSpec(memory_space=pltpu.SMEM)]
        + [pl.BlockSpec(memory_space=pl.ANY)] * 2
        + [pl.BlockSpec(memory_space=pltpu.VMEM)],
        out_specs=[pl.BlockSpec(memory_space=pltpu.VMEM)] * 2,
        scratch_shapes=[
            pltpu.VMEM(flat.shape, jnp.bfloat16),
            pltpu.VMEM(query_weight.shape, jnp.bfloat16),
            pltpu.VMEM((text_tokens // TEXT_CHUNKS, DEC), jnp.bfloat16),
            pltpu.SemaphoreType.DMA((TEXT_CHUNKS + 1,)),
        ],
        compiler_params=pltpu.CompilerParams(vmem_limit_bytes=8 << 20),
        name="query",
    )(
        (lax.axis_index(MP) * tokens_here).reshape(1),
        in_hbm(flat),
        in_hbm(query_weight),
        text_gain.reshape(1, DEC),
    )
    gain = vis_gain.reshape(rows, cols, features).transpose(1, 0, 2).reshape(cols, rows * features)
    column = pl.pallas_call(
        turn_kernel,
        out_shape=jax.ShapeDtypeStruct((halves * half_tokens, rows * features), jnp.bfloat16),
        in_specs=[pl.BlockSpec(memory_space=pltpu.VMEM)],
        out_specs=pl.BlockSpec(memory_space=pltpu.VMEM),
        compiler_params=pltpu.CompilerParams(vmem_limit_bytes=4 << 20),
        name="turn",
    )(in_vmem(column.reshape(halves, rows * features, half_tokens)))
    column = (column.astype(jnp.float32) * SCALE).astype(jnp.float16)
    whole = lax.all_gather(column, COL, axis=0, tiled=True)
    whole = whole.astype(jnp.bfloat16).reshape(cols, halves * half_tokens, rows * features)
    operands = [in_vmem(v) for v in (whole, gain, queries)]
    operands += [in_hbm(w.reshape(devices, features, HEAD_DIM)) for w in (key_weight, value_weight)]
    contexts = pl.pallas_call(
        attention_kernel,
        out_shape=jax.ShapeDtypeStruct((quad, text_tokens, HEAD_DIM), jnp.bfloat16),
        in_specs=[pl.BlockSpec(memory_space=pltpu.VMEM)] * 3 + [pl.BlockSpec(memory_space=pltpu.HBM)] * 2,
        out_specs=pl.BlockSpec(memory_space=pltpu.VMEM),
        scratch_shapes=[
            *(pltpu.VMEM(w.shape, jnp.bfloat16) for w in operands[3:]),
            pltpu.SemaphoreType.DMA((2,)),
            pltpu.VMEM(whole.shape, jnp.bfloat16),
            pltpu.VMEM((whole.shape[1], LANES), jnp.float32),
        ],
        compiler_params=pltpu.CompilerParams(vmem_limit_bytes=12 << 20),
        name="attention",
    )(*operands)
    contexts, member, *out_rows = lax.optimization_barrier((contexts, member.reshape(1), *out_rows))
    group = lax.all_to_all(contexts, QUAD, 0, 0, tiled=True)
    operands = [in_vmem(v) for v in (group, *out_rows)]
    part = pl.pallas_call(
        project_kernel,
        out_shape=jax.ShapeDtypeStruct((text_tokens, width), jnp.bfloat16),
        in_specs=[pl.BlockSpec(memory_space=pltpu.SMEM)] + [pl.BlockSpec(memory_space=pltpu.VMEM)] * len(operands),
        out_specs=pl.BlockSpec(memory_space=pltpu.VMEM),
        compiler_params=pltpu.CompilerParams(vmem_limit_bytes=12 << 20),
        name="project",
    )(member, *operands)
    parts = lax.all_to_all(part.reshape(devices, tokens_here, width), MP, 0, 0, tiled=True)
    parts = parts.reshape(*(lax.axis_size(a) for a in MP), tokens_here, width)
    mixed = pl.pallas_call(
        finish_kernel,
        out_shape=jax.ShapeDtypeStruct((tokens_here, DEC), jnp.bfloat16),
        in_specs=[pl.BlockSpec(memory_space=pltpu.VMEM)] * 2,
        out_specs=pl.BlockSpec(memory_space=pltpu.VMEM),
        compiler_params=pltpu.CompilerParams(vmem_limit_bytes=12 << 20),
        name="finish",
    )(in_vmem(parts), in_vmem(residual))
    return mixed.reshape(tokens_here, 1, DEC)


def solution(mesh):
    split = Mesh(mesh.devices.reshape(2, mesh.shape["dp"] // 2, 2, 2, 4, 2), DP + MP)
    in_specs = (
        P(DP, None, MP),
        P(),
        P(None, DP, None),
        P(),
        P(None, MP),
        P(None, MP),
        P(None, MP),
        P(MP, None),
    )
    out_specs = P(MP, DP, None)
    return jax.shard_map(attend, mesh=split, in_specs=in_specs, out_specs=out_specs, check_vma=False)
```
